512 devices in a mesh: mom: 128 (over y, z, core), tm: 4 (over x).
Axes of the slice: x: 4, y: 8, z: 8, core: 2. Of those that a mesh axis runs over, the one named last changes fastest.
Arguments:
- history: float32 [4, 128, 640, 1024], P(None, 'mom', None, 'tm'), may hold values from -6 to 6
- sigma_first: float32 [4, 128, 1024], P(None, None, 'tm'), may hold values from -4 to 4
- propagator: float32 [4, 128, 384], P(None, 'mom'), may hold values from -4 to 4
Outputs:
- green_last: float32 [4, 128, 128, 1024], P(None, 'mom', None, 'tm')
- sigma_next: float32 [4, 128, 1024], P(None, None, 'tm')
The draws below stay inside these ranges and needn't reach their ends.
All inputs are finite; a program needn't handle non-finite values.
Results may differ from the reference program's by a relative error of at most 0.0003.
Values sent between devices are 32-bit elements; how exact they have to be, the bound alone decides.
No kernel may reach another device: no remote copies, remote signals or barrier semaphores. Data moves between devices by JAX's collectives and lax.ppermute only.
A program may use at most 64 MiB of HBM per device.

```python
import jax
import jax.numpy as jnp
from jax import lax

NT = 1024
BLK = 128
NBLK = 3
MOMENTA = 128
HIST = 640
NEW = 384


def levels(key, shape, shards, smallest, top_value):
    def one(dim, blocks):
        draws = jax.random.uniform(jax.random.fold_in(jax.random.fold_in(key, 6), dim), (blocks,), jnp.float32, smallest / len(shards), top_value / len(shards))
        return jnp.repeat(jnp.exp(draws), shape[dim] // blocks).reshape((-1,) + (1,) * (len(shape) - dim - 1))

    gain = one(*shards[0])
    for cut in shards[1:]:
        gain = gain * one(*cut)
    return gain


def bell_draw(rng, extent, width, bound, pieces=(), kind=jnp.bfloat16):
    level = levels(rng, extent, pieces, -0.22, 0.18) if pieces else 1.0
    entries = jax.random.normal(rng, extent, jnp.float32) * width * level
    return jnp.minimum(jnp.maximum(entries, -bound), bound).astype(kind)


def setup_inputs(seed: int = 0) -> dict:
    keys = jax.random.split(jax.random.key(seed), 4)
    history = bell_draw(keys[0], (4, MOMENTA, HIST, NT), 1.0, 6.0, ((1, 128), (3, 4)), jnp.float32)
    sigma_first = bell_draw(keys[1], (4, BLK, NT), 0.3, 4.0, ((2, 4),), jnp.float32)
    propagator = bell_draw(keys[2], (4, MOMENTA, NEW), 0.6, 4.0, ((1, 128),), jnp.float32)
    return {"history": history, "sigma_first": sigma_first, "propagator": propagator}


def contract(sigma, rows):
    parts = []
    for orbital in range(2):
        s_re = sigma[2 * orbital]
        s_im = sigma[2 * orbital + 1]
        h_re = rows[2 * orbital]
        h_im = rows[2 * orbital + 1]
        hp = lax.Precision.HIGHEST
        real_part = jnp.einsum('tu,kus->kts', s_re, h_re, precision=hp) - jnp.einsum('tu,kus->kts', s_im, h_im, precision=hp)
        imag_part = jnp.einsum('tu,kus->kts', s_re, h_im, precision=hp) + jnp.einsum('tu,kus->kts', s_im, h_re, precision=hp)
        parts.append(real_part)
        parts.append(imag_part)
    return jnp.stack(parts)

def cubic(local):
    parts = []
    for orbital in range(2):
        a_part = local[2 * orbital]
        b_part = local[2 * orbital + 1]
        parts.append(0.1 * (a_part * a_part * a_part - 3.0 * a_part * b_part * b_part))
        parts.append(0.1 * (3.0 * a_part * a_part * b_part - b_part * b_part * b_part))
    return jnp.stack(parts)

def advance(previous, convolved, factor, row_ids, col_ids, step_size):
    inner = previous + step_size * convolved
    parts = []
    for orbital in range(2):
        p_re = factor[2 * orbital][:, :, None]
        p_im = factor[2 * orbital + 1][:, :, None]
        x_re = inner[2 * orbital]
        x_im = inner[2 * orbital + 1]
        parts.append(p_re * x_re - p_im * x_im)
        parts.append(p_re * x_im + p_im * x_re)
    keep = (col_ids[None, :] <= row_ids[:, None]).astype(jnp.float32)
    return jnp.stack(parts) * keep[None, None]

def reference(history, sigma_first, propagator):
    step_size = 1.0 / jnp.sqrt(jnp.float32(NT))
    col_ids = jnp.arange(NT, dtype=jnp.int32)
    hist_rows = jnp.arange(HIST, dtype=jnp.int32)
    known = history * (col_ids[None, :] <= hist_rows[:, None]).astype(jnp.float32)[None, None]
    window = jnp.zeros((4, MOMENTA, NEW, NT), jnp.float32)
    sigma = sigma_first
    green = None
    for block in range(NBLK):
        start = HIST + block * BLK
        convolved = contract(sigma[:, :, :HIST], known) + contract(sigma[:, :, HIST:], window)
        if block == 0:
            previous = known[:, :, HIST - BLK:HIST, :]
        else:
            previous = window[:, :, start - BLK - HIST:start - HIST, :]
        row_ids = start + jnp.arange(BLK, dtype=jnp.int32)
        factor = propagator[:, :, block * BLK:(block + 1) * BLK]
        green = advance(previous, convolved, factor, row_ids, col_ids, step_size)
        window = window.at[:, :, block * BLK:(block + 1) * BLK, :].set(green)
        local = lax.optimization_barrier(jnp.sum(green, axis=1)) / jnp.sqrt(jnp.float32(MOMENTA))
        sigma = cubic(local)
    return (green, sigma)
```

```python
import functools

import jax
import jax.numpy as jnp
from jax import lax
from jax.experimental import pallas as pl
from jax.experimental.pallas import tpu as pltpu
from jax.sharding import Mesh
from jax.sharding import PartitionSpec as P

GRID = (8, 8, 2)
CORE = "core_of_chip"
YZ = ("mom_0", "mom_1")
SUB = 4
LANES = 128


def halves_of(value):
    high = value.astype(jnp.bfloat16)
    return high, (value - high.astype(jnp.float32)).astype(jnp.bfloat16)


def packed(real, imag):
    top = lax.broadcasted_iota(jnp.int32, real.shape, 0) < SUB
    return jnp.where(top, real, jnp.roll(imag, SUB, 0)), jnp.where(top, jnp.roll(real, SUB, 0), imag)


def store_packed(store, real, imag):
    rows, cols = real.shape
    wide = cols // LANES
    for pair in range(rows // 8):
        for h in range(wide):
            window = (slice(8 * pair, 8 * pair + 8), slice(LANES * h, LANES * h + LANES))
            first, second = packed(real[window], imag[window])
            store((2 * pair) * wide + h, first)
            store((2 * pair + 1) * wide + h, second)


def pack_kernel(place, sigma_ref, out_ref):
    copies, rows = out_ref.shape[0], sigma_ref.shape[1] // 2
    mine = pl.ds(pl.multiple_of(place[1] * rows, 8), rows)

    def store(index, tile):
        for copy in range(copies):
            out_ref[copy, index] = tile

    store_packed(store, sigma_ref[0, mine, :], sigma_ref[1, mine, :])


def pack(place, sigma, copies):
    comps, rows, cols = sigma.shape
    pieces = (rows // 2) * cols // (SUB * LANES)
    return pl.pallas_call(
        pack_kernel,
        out_shape=jax.ShapeDtypeStruct((copies, comps // 2 * pieces, 8, LANES), jnp.float32),
        grid_spec=pltpu.PrefetchScalarGridSpec(
            num_scalar_prefetch=1,
            grid=(comps // 2,),
            in_specs=[pl.BlockSpec((2, rows, cols), lambda o, p: (o, 0, 0))],
            out_specs=pl.BlockSpec((copies, pieces, 8, LANES), lambda o, p: (0, o, 0, 0)),
        ),
        name="pack",
    )(place, sigma)


def split_kernel(place, history_ref, high_ref, low_ref, last_ref):
    _, rows, cols = history_ref.shape
    keep_rows = last_ref.shape[1]
    col_ids = place[0] * cols + lax.broadcasted_iota(jnp.int32, (rows, cols), 1)
    keep = col_ids <= lax.broadcasted_iota(jnp.int32, (rows, cols), 0)
    known = jnp.where(keep, history_ref[0], 0.0)
    high, low = halves_of(known)
    high_ref[0] = high
    low_ref[0] = low
    start = rows - 2 * keep_rows + place[1] * keep_rows
    row_ids = start + lax.broadcasted_iota(jnp.int32, (keep_rows, cols), 0)
    mine = pl.ds(pl.multiple_of(start, 8), keep_rows)
    last_ref[0] = jnp.where(col_ids[:keep_rows] <= row_ids, history_ref[0, mine, :], 0.0)


def split(place, history, keep_rows):
    comps, rows, cols = history.shape
    return pl.pallas_call(
        split_kernel,
        out_shape=(
            jax.ShapeDtypeStruct(history.shape, jnp.bfloat16),
            jax.ShapeDtypeStruct(history.shape, jnp.bfloat16),
            jax.ShapeDtypeStruct((comps, keep_rows, cols), jnp.float32),
        ),
        grid_spec=pltpu.PrefetchScalarGridSpec(
            num_scalar_prefetch=1,
            grid=(comps,),
            in_specs=[pl.BlockSpec((1, rows, cols), lambda i, p: (i, 0, 0))],
            out_specs=(
                pl.BlockSpec((1, rows, cols), lambda i, p: (i, 0, 0)),
                pl.BlockSpec((1, rows, cols), lambda i, p: (i, 0, 0)),
                pl.BlockSpec((1, keep_rows, cols), lambda i, p: (i, 0, 0)),
            ),
        ),
        name="split",
    )(place, history)


def block_kernel(block, windows, step_size, place, *refs):
    sigma_ref, factor_ref, highs, lows, previous = refs[0], refs[1], refs[2:4], refs[4:6], refs[6:8]
    mine_refs, theirs_refs = refs[8 : 8 + 2 * windows], refs[8 + 2 * windows : 8 + 4 * windows]
    green_refs = refs[8 + 4 * windows : 10 + 4 * windows]
    piece_ref, sigma_scratch, joined = refs[10 + 4 * windows :]
    orbital = pl.program_id(0)
    rows, cols = previous[0].shape[1:]
    known_rows = highs[0].shape[1]
    used = known_rows + windows * 2 * rows
    wide = cols // LANES
    top = lax.broadcasted_iota(jnp.int32, (8, LANES), 0) < SUB
    for tile in range(pl.cdiv(used, LANES)):
        shard, h = tile // wide, tile % wide
        reals, imags = [], []
        for pair in range(rows // 8):
            first = sigma_ref[shard, (2 * pair) * wide + h]
            second = sigma_ref[shard, (2 * pair + 1) * wide + h]
            reals.append(jnp.where(top, first, jnp.roll(second, SUB, 0)))
            imags.append(jnp.where(top, jnp.roll(first, SUB, 0), second))
        high, low = halves_of(jnp.concatenate(reals + imags, 0))
        lanes = slice(LANES * tile, LANES * tile + LANES)
        sigma_scratch[: 2 * rows, lanes] = high
        sigma_scratch[2 * rows :, lanes] = low

    def product(span, high, low):
        both = jnp.dot(sigma_scratch[:, span], high, preferred_element_type=jnp.float32)
        rest = jnp.dot(sigma_scratch[: 2 * rows, span], low, preferred_element_type=jnp.float32)
        return both[: 2 * rows] + (both[2 * rows :] + rest)

    row_ids = known_rows + block * 2 * rows + place[1] * rows + lax.broadcasted_iota(jnp.int32, (rows, cols), 0)
    keep = place[0] * cols + lax.broadcasted_iota(jnp.int32, (rows, cols), 1) <= row_ids
    totals = None
    for momentum in range(2):
        products = []
        for part in range(2):
            total = product(slice(0, known_rows), highs[momentum][part], lows[momentum][part])
            for window in range(windows):
                joined[pl.ds(pl.multiple_of(place[1] * rows, 8), rows), :] = mine_refs[2 * window + momentum][part]
                joined[pl.ds(pl.multiple_of((1 - place[1]) * rows, 8), rows), :] = theirs_refs[2 * window + momentum][part]
                start = known_rows + window * 2 * rows
                total = total + product(slice(start, start + 2 * rows), *halves_of(joined[...]))
            products.append(total)
        by_real, by_imag = products
        x_re = previous[momentum][0] + step_size * (by_real[:rows] - by_imag[rows:])
        x_im = previous[momentum][1] + step_size * (by_imag[:rows] + by_real[rows:])
        p_re = factor_ref[0, :, momentum : momentum + 1]
        p_im = factor_ref[0, :, 2 + momentum : 3 + momentum]
        real = jnp.where(keep, p_re * x_re - p_im * x_im, 0.0)
        imag = jnp.where(keep, p_re * x_im + p_im * x_re, 0.0)
        green_refs[momentum][0] = real
        green_refs[momentum][1] = imag
        totals = (real, imag) if totals is None else (totals[0] + real, totals[1] + imag)

    def store(index, tile):
        piece_ref[index] = tile

    store_packed(store, *totals)


def advance(place, block, step_size, sigma, factor, highs, lows, previous, windows):
    comps, rows, cols = previous[0].shape
    known_rows = highs[0].shape[1]
    shards, pieces = sigma.shape[:2]
    mine = [array for pair, _ in windows for array in pair]
    theirs = [array for _, pair in windows for array in pair]
    known = pl.BlockSpec((2, known_rows, cols), lambda o, p: (o, 0, 0))
    small = pl.BlockSpec((2, rows, cols), lambda o, p: (o, 0, 0))
    used = known_rows + len(windows) * 2 * rows
    own, other, out = pl.pallas_call(
        functools.partial(block_kernel, block, len(windows), step_size),
        out_shape=(
            jax.ShapeDtypeStruct((comps, rows, cols), jnp.float32),
            jax.ShapeDtypeStruct((comps, rows, cols), jnp.float32),
            jax.ShapeDtypeStruct((pieces, 8, LANES), jnp.float32),
        ),
        grid_spec=pltpu.PrefetchScalarGridSpec(
            num_scalar_prefetch=1,
            grid=(comps // 2,),
            in_specs=[
                pl.BlockSpec((shards, pieces // 2, 8, LANES), lambda o, p: (0, o, 0, 0)),
                pl.BlockSpec((1, rows, 4), lambda o, p: (o, 0, 0)),
                known, known, known, known, small, small,
                *[small] * (4 * len(windows)),
            ],
            out_specs=(small, small, pl.BlockSpec((pieces // 2, 8, LANES), lambda o, p: (o, 0, 0))),
            scratch_shapes=[
                pltpu.VMEM((4 * rows, pl.cdiv(used, LANES) * LANES), jnp.bfloat16),
                pltpu.VMEM((2 * rows, cols), jnp.float32),
            ],
        ),
        name=f"block_{block}",
    )(place, sigma, factor, *highs, *lows, *previous, *mine, *theirs)
    return (own, other), out


def cube_kernel(norm_factor, parts_ref, out_ref):
    local = jnp.sum(parts_ref[...], axis=0) * norm_factor
    paired = jnp.roll(local, SUB, 0)
    value = 0.1 * (local * local * local - 3.0 * local * paired * paired)
    top = lax.broadcasted_iota(jnp.int32, local.shape, 0) < SUB
    out_ref[...] = jnp.broadcast_to(jnp.where(top, value, -value), out_ref.shape)


def cube(parts, norm_factor):
    return pl.pallas_call(
        functools.partial(cube_kernel, norm_factor),
        out_shape=jax.ShapeDtypeStruct(parts.shape, jnp.float32),
        name="cube",
    )(parts)


def finish_kernel(place, green_ref, their_green_ref, sigma_ref, their_sigma_ref, green_out, sigma_out):
    comps, rows, cols = green_ref.shape
    wide = cols // LANES
    mine = pl.multiple_of(place[1] * rows, 8)
    theirs = pl.multiple_of((1 - place[1]) * rows, 8)
    green_out[:, pl.ds(mine, rows), :] = green_ref[...]
    green_out[:, pl.ds(theirs, rows), :] = their_green_ref[...]
    top = lax.broadcasted_iota(jnp.int32, (8, LANES), 0) < SUB
    per_orbital = sigma_ref.shape[0] // (comps // 2)
    for start, ref in ((mine, sigma_ref), (theirs, their_sigma_ref)):
        for orbital in range(comps // 2):
            for pair in range(rows // 8):
                at = pl.ds(pl.multiple_of(start + 8 * pair, 8), 8)
                for h in range(wide):
                    first = ref[orbital * per_orbital + (2 * pair) * wide + h]
                    second = ref[orbital * per_orbital + (2 * pair + 1) * wide + h]
                    lanes = slice(LANES * h, LANES * h + LANES)
                    sigma_out[2 * orbital, at, lanes] = jnp.where(top, first, jnp.roll(second, SUB, 0))
                    sigma_out[2 * orbital + 1, at, lanes] = jnp.where(top, jnp.roll(first, SUB, 0), second)


def finish(place, green, their_green, sigma, their_sigma):
    comps, rows, cols = green.shape
    whole = jax.ShapeDtypeStruct((comps, 2 * rows, cols), jnp.float32)
    vmem = pl.BlockSpec(memory_space=pltpu.VMEM)
    return pl.pallas_call(
        finish_kernel,
        out_shape=(whole, whole),
        in_specs=[pl.BlockSpec(memory_space=pltpu.SMEM), vmem, vmem, vmem, vmem],
        out_specs=(vmem, vmem),
        name="finish",
    )(place, green, their_green, sigma, their_sigma)


def body(history, sigma_first, propagator):
    history, propagator = history[:, 0], propagator[:, 0]
    comps, hist_rows, cols = history.shape
    rows_block = sigma_first.shape[1]
    blocks = propagator.shape[1] // rows_block
    rows = rows_block // 2
    shards = lax.axis_size("tm")
    step_size = 1.0 / float(cols * shards) ** 0.5
    norm_factor = 1.0 / float(lax.axis_size(YZ) * lax.axis_size(CORE)) ** 0.5
    core = lax.axis_index(CORE)
    place = jnp.stack([lax.axis_index("tm"), core]).astype(jnp.int32)

    def swapped(value):
        return lax.ppermute(value, CORE, [(0, 1), (1, 0)])

    sigma = lax.all_to_all(pack(place, sigma_first, shards), "tm", 0, 0, tiled=True)
    their_history = swapped(history)
    their_propagator = swapped(propagator)
    own = split(place, history, rows)
    other = split(place, their_history, rows)
    highs, lows, green = (own[0], other[0]), (own[1], other[1]), (own[2], other[2])
    factors = jnp.stack([propagator, their_propagator]).reshape(2, comps // 2, 2, blocks, 2, rows)
    factors = lax.dynamic_index_in_dim(factors, core, 4, keepdims=False)
    factors = factors.transpose(3, 1, 4, 2, 0).reshape(blocks, comps // 2, rows, 4)
    windows = []
    for block in range(blocks):
        green, pieces = advance(place, block, step_size, sigma, factors[block], highs, lows, green, windows)
        last = block + 1 == blocks
        if last:
            their_green = swapped(green[1])
        else:
            theirs = swapped(jnp.stack(green[::-1]))
            windows.append((green, (theirs[0], theirs[1])))
        parts = lax.all_to_all(pieces, YZ, 0, 0, tiled=True)
        sigma = lax.all_to_all(cube(parts, norm_factor), YZ, 0, 0, tiled=True)
        if not last:
            copies = jnp.broadcast_to(sigma, (shards, *sigma.shape))
            sigma = lax.all_to_all(copies, "tm", 0, 0, tiled=True)
    green_last, sigma_next = finish(place, green[0], their_green, sigma, swapped(sigma))
    return green_last[:, None], sigma_next


def solution(mesh):
    torus = Mesh(mesh.devices.reshape(*GRID, mesh.shape["tm"]), (*YZ, CORE, "tm"))
    moms = (*YZ, CORE)
    return jax.shard_map(
        body,
        mesh=torus,
        in_specs=(P(None, moms, None, "tm"), P(None, None, "tm"), P(None, moms, None)),
        out_specs=(P(None, moms, None, "tm"), P(None, None, "tm")),
        check_vma=False,
    )
```

```python
import functools

import jax
import jax.numpy as jnp
from jax import lax
from jax.experimental import pallas as pl
from jax.experimental.pallas import tpu as pltpu
from jax.sharding import Mesh
from jax.sharding import PartitionSpec as P


GRID = (8, 8, 2)
CORE = "core_of_chip"
YZ = ("mom_0", "mom_1")
VMEM_LIMIT = 32 << 20
SUB = 4
LANES = 128


def near(value):
    return pltpu.with_memory_space_constraint(value, pltpu.VMEM)


def far(value):
    return pltpu.with_memory_space_constraint(value, pltpu.HBM)


def near_out(shape, dtype=jnp.float32):
    return pltpu.VMEM(shape, dtype)


def far_out(shape, dtype=jnp.float32):
    return pltpu.HBM(shape, dtype)


def call(kernel, inputs, outputs, scratch=()):
    vmem = pl.BlockSpec(memory_space=pltpu.VMEM)
    return pl.pallas_call(
        kernel,
        out_shape=tuple(outputs),
        in_specs=[vmem] * len(inputs),
        out_specs=(vmem,) * len(outputs),
        scratch_shapes=scratch,
        compiler_params=pltpu.CompilerParams(vmem_limit_bytes=VMEM_LIMIT),
    )(*[near(value) for value in inputs])


def halves_of(value):
    high = value.astype(jnp.bfloat16)
    return high, (value - high.astype(jnp.float32)).astype(jnp.bfloat16)


def packed(real, imag):
    top = lax.broadcasted_iota(jnp.int32, real.shape, 0) < SUB
    return jnp.where(top, real, jnp.roll(imag, SUB, 0)), jnp.where(top, jnp.roll(real, SUB, 0), imag)


def store_packed(store, real, imag):
    rows, cols = real.shape
    wide = cols // LANES
    for pair in range(rows // 8):
        for h in range(wide):
            window = (slice(8 * pair, 8 * pair + 8), slice(LANES * h, LANES * h + LANES))
            first, second = packed(real[window], imag[window])
            store((2 * pair) * wide + h, first)
            store((2 * pair + 1) * wide + h, second)


def pack_kernel(sigma_ref, out_ref):
    copies, pieces = out_ref.shape[:2]
    comps, rows = sigma_ref.shape[0], sigma_ref.shape[1] // 2
    mine = pl.ds(pl.multiple_of(lax.axis_index(CORE) * rows, 8), rows)

    for orbital in range(comps // 2):

        def store(index, tile, orbital=orbital):
            for copy in range(copies):
                out_ref[copy, orbital * (pieces // (comps // 2)) + index] = tile

        store_packed(store, sigma_ref[2 * orbital, mine, :], sigma_ref[2 * orbital + 1, mine, :])


def pack(sigma, copies):
    comps, rows, cols = sigma.shape
    pieces = comps // 2 * (rows // 2) * cols // (SUB * LANES)
    return call(pack_kernel, [sigma], [far_out((copies, pieces, 8, LANES))])[0]


def split_kernel(history_ref, high_ref, low_ref, last_ref):
    _, rows, cols = history_ref.shape
    keep_rows = last_ref.shape[1]
    col_ids = lax.axis_index("tm") * cols + lax.broadcasted_iota(jnp.int32, (rows, cols), 1)
    keep = col_ids <= lax.broadcasted_iota(jnp.int32, (rows, cols), 0)
    high, low = halves_of(jnp.where(keep, history_ref[0], 0.0))
    high_ref[0] = high
    low_ref[0] = low
    start = rows - 2 * keep_rows + lax.axis_index(CORE) * keep_rows
    row_ids = start + lax.broadcasted_iota(jnp.int32, (keep_rows, cols), 0)
    mine = pl.ds(pl.multiple_of(start, 8), keep_rows)
    last_ref[0] = jnp.where(col_ids[:keep_rows] <= row_ids, history_ref[0, mine, :], 0.0)


def split(history, keep_rows):
    comps, rows, cols = history.shape
    whole = pl.BlockSpec((1, rows, cols), lambda i: (i, 0, 0))
    return pl.pallas_call(
        split_kernel,
        out_shape=(
            far_out(history.shape, jnp.bfloat16),
            far_out(history.shape, jnp.bfloat16),
            far_out((comps, keep_rows, cols)),
        ),
        grid=(comps,),
        in_specs=[whole],
        out_specs=(whole, whole, pl.BlockSpec((1, keep_rows, cols), lambda i: (i, 0, 0))),
        compiler_params=pltpu.CompilerParams(vmem_limit_bytes=VMEM_LIMIT),
        name="split",
    )(far(history))


def block_kernel(block, windows, stacked, step_size, *refs):
    count = 4 + (1 if stacked else 2) + 2 * windows
    factor_ref, sigma_ref, sources = refs[0], refs[1], refs[2 : 2 + count]
    outs, buffers, arrived = refs[2 + count : -(count + 3)], refs[-(count + 3) : -3], refs[-3]
    piece_ref, outs = outs[-1], outs[:-1]
    sigma_scratch, joined = refs[-2:]
    highs, lows = buffers[:2], buffers[2:4]
    previous = (buffers[4].at[0], buffers[4].at[1]) if stacked else buffers[4:6]
    mine_refs, theirs_refs = buffers[-2 * windows : count - windows], buffers[count - windows :]
    comps, rows, cols = previous[0].shape
    orbitals = comps // 2
    known_rows = highs[0].shape[1]
    used = known_rows + windows * 2 * rows
    wide = cols // LANES
    per_orbital = piece_ref.shape[0] // orbitals

    def part_of(ref, orbital):
        span = pl.ds(2 * orbital, 2)
        return ref.at[span] if len(ref.shape) == 3 else ref.at[:, span]

    copies = [
        [
            pltpu.make_async_copy(part_of(source, o), part_of(buffer, o), arrived.at[o, i])
            for i, (source, buffer) in enumerate(zip(sources, buffers, strict=True))
        ]
        for o in range(orbitals)
    ]
    for of_orbital in copies:
        for copy in of_orbital:
            copy.start()
    core = lax.axis_index(CORE)
    mine_at = pl.ds(pl.multiple_of(core * rows, 8), rows)
    theirs_at = pl.ds(pl.multiple_of((1 - core) * rows, 8), rows)
    top = lax.broadcasted_iota(jnp.int32, (8, LANES), 0) < SUB
    row_ids = known_rows + block * 2 * rows + core * rows + lax.broadcasted_iota(jnp.int32, (rows, cols), 0)
    keep = lax.axis_index("tm") * cols + lax.broadcasted_iota(jnp.int32, (rows, cols), 1) <= row_ids

    def product(span, high, low):
        both = jnp.dot(sigma_scratch[:, span], high, preferred_element_type=jnp.float32)
        rest = jnp.dot(sigma_scratch[: 2 * rows, span], low, preferred_element_type=jnp.float32)
        return both[: 2 * rows] + (both[2 * rows :] + rest)

    for orbital in range(orbitals):
        base = orbital * per_orbital
        for tile in range(pl.cdiv(used, LANES)):
            shard, h = tile // wide, tile % wide
            reals, imags = [], []
            for pair in range(rows // 8):
                first = sigma_ref[shard, base + (2 * pair) * wide + h]
                second = sigma_ref[shard, base + (2 * pair + 1) * wide + h]
                reals.append(jnp.where(top, first, jnp.roll(second, SUB, 0)))
                imags.append(jnp.where(top, jnp.roll(first, SUB, 0), second))
            high, low = halves_of(jnp.concatenate(reals + imags, 0))
            lanes = slice(LANES * tile, LANES * tile + LANES)
            sigma_scratch[: 2 * rows, lanes] = high
            sigma_scratch[2 * rows :, lanes] = low
        for copy in copies[orbital]:
            copy.wait()

        totals = None
        for momentum in range(2):
            products = []
            for part in range(2 * orbital, 2 * orbital + 2):
                total = product(slice(0, known_rows), highs[momentum][part], lows[momentum][part])
                for window in range(windows):
                    joined[mine_at, :] = mine_refs[window][momentum, part]
                    joined[theirs_at, :] = theirs_refs[window][1 - momentum, part]
                    start = known_rows + window * 2 * rows
                    total = total + product(slice(start, start + 2 * rows), *halves_of(joined[...]))
                products.append(total)
            by_real, by_imag = products
            x_re = previous[momentum][2 * orbital] + step_size * (by_real[:rows] - by_imag[rows:])
            x_im = previous[momentum][2 * orbital + 1] + step_size * (by_imag[:rows] + by_real[rows:])
            p_re = factor_ref[block, orbital, :, momentum : momentum + 1]
            p_im = factor_ref[block, orbital, :, 2 + momentum : 3 + momentum]
            real = jnp.where(keep, p_re * x_re - p_im * x_im, 0.0)
            imag = jnp.where(keep, p_re * x_im + p_im * x_re, 0.0)
            out = outs[0].at[momentum] if len(outs) == 1 else outs[momentum]
            out[2 * orbital] = real
            out[2 * orbital + 1] = imag
            totals = (real, imag) if totals is None else (totals[0] + real, totals[1] + imag)

        def store(index, tile, base=base):
            piece_ref[base + index] = tile

        store_packed(store, *totals)


def advance(block, last, step_size, sigma, factors, highs, lows, previous, mine, theirs):
    comps, known_rows, cols = highs[0].shape
    rows = factors.shape[2]
    used = pl.cdiv(known_rows + len(mine) * 2 * rows, LANES) * LANES
    sources = [*highs, *lows, *previous, *mine, *theirs]
    greens = [far_out((comps, rows, cols))] * 2 if last else [far_out((2, comps, rows, cols))]
    vmem = pl.BlockSpec(memory_space=pltpu.VMEM)
    *greens, pieces = pl.pallas_call(
        functools.partial(block_kernel, block, len(mine), len(previous) == 1, step_size),
        out_shape=(*greens, near_out((sigma.shape[1], 8, LANES))),
        in_specs=[vmem, vmem] + [pl.BlockSpec(memory_space=pl.ANY)] * len(sources),
        out_specs=(vmem,) * (len(greens) + 1),
        scratch_shapes=[
            *[pltpu.VMEM(source.shape, source.dtype) for source in sources],
            pltpu.SemaphoreType.DMA((comps // 2, len(sources))),
            pltpu.VMEM((4 * rows, used), jnp.bfloat16),
            pltpu.VMEM((2 * rows, cols), jnp.float32),
        ],
        compiler_params=pltpu.CompilerParams(vmem_limit_bytes=VMEM_LIMIT),
    )(factors, near(sigma), *[far(source) for source in sources])
    return greens, pieces


def cube_kernel(norm_factor, parts_ref, out_ref):
    sums = [parts_ref[i] for i in range(4)]
    for i in range(4, parts_ref.shape[0]):
        sums[i % 4] = sums[i % 4] + parts_ref[i]
    local = ((sums[0] + sums[1]) + (sums[2] + sums[3])) * norm_factor
    paired = jnp.roll(local, SUB, 0)
    value = 0.1 * (local * local * local - 3.0 * local * paired * paired)
    top = lax.broadcasted_iota(jnp.int32, local.shape, 0) < SUB
    value = jnp.where(top, value, -value)
    for i in range(out_ref.shape[0]):
        out_ref[i] = value


def cube(parts, norm_factor):
    kernel = functools.partial(cube_kernel, norm_factor)
    return call(kernel, [parts], [near_out(parts.shape)])[0]


def copies_kernel(value_ref, out_ref):
    for i in range(out_ref.shape[0]):
        out_ref[i] = value_ref[...]


def copies_of(value, count):
    return call(copies_kernel, [value], [far_out((count, *value.shape))])[0]


def green_kernel(mine_ref, theirs_ref, out_ref):
    rows = mine_ref.shape[1]
    core = lax.axis_index(CORE)
    out_ref[:, pl.ds(pl.multiple_of(core * rows, 8), rows), :] = mine_ref[...]
    out_ref[:, pl.ds(pl.multiple_of((1 - core) * rows, 8), rows), :] = theirs_ref[...]


def sigma_kernel(mine_ref, theirs_ref, out_ref):
    comps, rows, cols = out_ref.shape
    rows = rows // 2
    wide = cols // LANES
    core = lax.axis_index(CORE)
    top = lax.broadcasted_iota(jnp.int32, (8, LANES), 0) < SUB
    per_orbital = mine_ref.shape[0] // (comps // 2)
    for start, ref in ((core * rows, mine_ref), ((1 - core) * rows, theirs_ref)):
        for orbital in range(comps // 2):
            for pair in range(rows // 8):
                at = pl.ds(pl.multiple_of(start + 8 * pair, 8), 8)
                for h in range(wide):
                    first = ref[orbital * per_orbital + (2 * pair) * wide + h]
                    second = ref[orbital * per_orbital + (2 * pair + 1) * wide + h]
                    lanes = slice(LANES * h, LANES * h + LANES)
                    out_ref[2 * orbital, at, lanes] = jnp.where(top, first, jnp.roll(second, SUB, 0))
                    out_ref[2 * orbital + 1, at, lanes] = jnp.where(top, jnp.roll(first, SUB, 0), second)


def body(history, sigma_first, propagator):
    history, propagator = history[:, 0], propagator[:, 0]
    comps, _, cols = history.shape
    rows_block = sigma_first.shape[1]
    blocks = propagator.shape[1] // rows_block
    rows = rows_block // 2
    shards = lax.axis_size("tm")
    step_size = 1.0 / float(cols * shards) ** 0.5
    norm_factor = 1.0 / float(lax.axis_size(YZ) * lax.axis_size(CORE)) ** 0.5
    core = lax.axis_index(CORE)

    def swapped(value):
        return lax.ppermute(value, CORE, [(0, 1), (1, 0)])

    packed_first = pack(sigma_first, shards)
    sigma = lax.all_to_all(packed_first, "tm", 0, 0, tiled=True)
    their_history = swapped(history)
    their_propagator = swapped(propagator)
    own = split(history, rows)
    other = split(their_history, rows)
    highs, lows, greens = (own[0], other[0]), (own[1], other[1]), (own[2], other[2])
    factors = jnp.stack([propagator, their_propagator]).reshape(2, comps // 2, 2, blocks, 2, rows)
    factors = lax.dynamic_index_in_dim(factors, core, 4, keepdims=False)
    factors = factors.transpose(3, 1, 4, 2, 0).reshape(blocks, comps // 2, rows, 4)
    mine, theirs = [], []
    for block in range(blocks):
        last = block + 1 == blocks
        greens, pieces = advance(block, last, step_size, sigma, factors, highs, lows, greens, mine, theirs)
        parts = lax.all_to_all(pieces, YZ, 0, 0, tiled=True)
        sigma = lax.all_to_all(cube(parts, norm_factor), YZ, 0, 0, tiled=True)
        if not last:
            mine.append(greens[0])
            theirs.append(swapped(greens[0]))
            sigma = lax.all_to_all(copies_of(sigma, shards), "tm", 0, 0, tiled=True)
    whole = [far_out((comps, rows_block, cols))]
    green_last = call(green_kernel, [greens[0], swapped(greens[1])], whole)[0]
    sigma_next = call(sigma_kernel, [sigma, swapped(sigma)], whole)[0]
    return green_last[:, None], sigma_next


def solution(mesh):
    torus = Mesh(mesh.devices.reshape(*GRID, mesh.shape["tm"]), (*YZ, CORE, "tm"))
    moms = (*YZ, CORE)
    return jax.shard_map(
        body,
        mesh=torus,
        in_specs=(P(None, moms, None, "tm"), P(None, None, "tm"), P(None, moms, None)),
        out_specs=(P(None, moms, None, "tm"), P(None, None, "tm")),
        check_vma=False,
    )
```

```python
import functools

import jax
import jax.numpy as jnp
from jax import lax
from jax.experimental import pallas as pl
from jax.experimental.pallas import tpu as pltpu
from jax.sharding import Mesh
from jax.sharding import PartitionSpec as P


GRID = (8, 8, 2)
CORE = "core_of_chip"
YZ = ("mom_0", "mom_1")
VMEM_LIMIT = 32 << 20
SUB = 4
LANES = 128


def near(value):
    return pltpu.with_memory_space_constraint(value, pltpu.VMEM)


def far(value):
    return pltpu.with_memory_space_constraint(value, pltpu.HBM)


def near_out(shape, dtype=jnp.float32):
    return pltpu.VMEM(shape, dtype)


def far_out(shape, dtype=jnp.float32):
    return pltpu.HBM(shape, dtype)


def call(kernel, inputs, outputs, scratch=()):
    vmem = pl.BlockSpec(memory_space=pltpu.VMEM)
    return pl.pallas_call(
        kernel,
        out_shape=tuple(outputs),
        in_specs=[vmem] * len(inputs),
        out_specs=(vmem,) * len(outputs),
        scratch_shapes=scratch,
        compiler_params=pltpu.CompilerParams(vmem_limit_bytes=VMEM_LIMIT),
    )(*[near(value) for value in inputs])


def halves_of(value):
    high = value.astype(jnp.bfloat16)
    return high, (value - high.astype(jnp.float32)).astype(jnp.bfloat16)


def packed(real, imag):
    top = lax.broadcasted_iota(jnp.int32, real.shape, 0) < SUB
    return jnp.where(top, real, jnp.roll(imag, SUB, 0)), jnp.where(top, jnp.roll(real, SUB, 0), imag)


def store_packed(store, real, imag):
    rows, cols = real.shape
    wide = cols // LANES
    for pair in range(rows // 8):
        for h in range(wide):
            window = (slice(8 * pair, 8 * pair + 8), slice(LANES * h, LANES * h + LANES))
            first, second = packed(real[window], imag[window])
            store((2 * pair) * wide + h, first)
            store((2 * pair + 1) * wide + h, second)


def send_copies(source, out_ref, sent, index, span):
    copies = [
        pltpu.make_async_copy(source.at[span], out_ref.at[copy, span], sent.at[index, copy])
        for copy in range(out_ref.shape[0])
    ]
    for copy in copies:
        copy.start()
    return copies


def pack_kernel(sigma_ref, out_ref, rows_buffer, piece_buffer, arrived, sent):
    comps, rows = rows_buffer.shape[:2]
    per_orbital = piece_buffer.shape[0] // (comps // 2)
    mine = pl.ds(pl.multiple_of(lax.axis_index(CORE) * rows, 8), rows)
    coming = [
        pltpu.make_async_copy(sigma_ref.at[pl.ds(2 * o, 2), mine], rows_buffer.at[pl.ds(2 * o, 2)], arrived.at[o])
        for o in range(comps // 2)
    ]
    for copy in coming:
        copy.start()
    going = []
    for orbital in range(comps // 2):
        coming[orbital].wait()

        def store(index, tile, orbital=orbital):
            piece_buffer[orbital * per_orbital + index] = tile

        store_packed(store, rows_buffer[2 * orbital], rows_buffer[2 * orbital + 1])
        going += send_copies(piece_buffer, out_ref, sent, orbital, pl.ds(orbital * per_orbital, per_orbital))
    for copy in going:
        copy.wait()


def pack(sigma, copies):
    comps, rows, cols = sigma.shape
    pieces = comps // 2 * (rows // 2) * cols // (SUB * LANES)
    anywhere = pl.BlockSpec(memory_space=pl.ANY)
    return pl.pallas_call(
        pack_kernel,
        out_shape=far_out((copies, pieces, 8, LANES)),
        in_specs=[anywhere],
        out_specs=anywhere,
        scratch_shapes=[
            pltpu.VMEM((comps, rows // 2, cols), jnp.float32),
            pltpu.VMEM((pieces, 8, LANES), jnp.float32),
            pltpu.SemaphoreType.DMA((comps // 2,)),
            pltpu.SemaphoreType.DMA((comps // 2, copies)),
        ],
        compiler_params=pltpu.CompilerParams(vmem_limit_bytes=VMEM_LIMIT),
        name="pack",
    )(far(sigma))


def split_kernel(resident, history_ref, *refs):
    comps, rows, cols = history_ref.shape
    orbitals = comps // 2
    outs, last_ref = refs[: 2 * orbitals], refs[2 * orbitals]
    away = [i for i in range(2 * orbitals) if i not in resident]
    buffer, *scratch, arrived, sent, sent_last = refs[2 * orbitals + 1 :]
    last_buffer = scratch.pop()
    places = list(outs)
    for i, ref in zip(away, scratch, strict=True):
        places[i] = ref
    keep_rows = last_ref.shape[1]
    chunk = arrived.shape[0]
    step = rows // chunk
    coming = []
    for c in range(chunk):
        span = (slice(None), pl.ds(c * step, step))
        coming.append(pltpu.make_async_copy(history_ref.at[span], buffer.at[span], arrived.at[c]))
        coming[-1].start()
    col_ids = lax.axis_index("tm") * cols + lax.broadcasted_iota(jnp.int32, (16, cols), 1)
    base_ids = lax.broadcasted_iota(jnp.int32, (16, cols), 0)
    going = []
    for c in range(chunk):
        coming[c].wait()
        for r in range(c * step, (c + 1) * step, 16):
            keep = col_ids <= r + base_ids
            for i in range(comps):
                high, low = halves_of(jnp.where(keep, buffer[i, r : r + 16, :], 0.0))
                places[2 * (i // 2)][i % 2, r : r + 16, :] = high
                places[2 * (i // 2) + 1][i % 2, r : r + 16, :] = low
        for n, i in enumerate(away):
            span = (slice(None), pl.ds(c * step, step))
            going.append(pltpu.make_async_copy(places[i].at[span], outs[i].at[span], sent.at[c, n]))
            going[-1].start()
    start = rows - 2 * keep_rows + lax.axis_index(CORE) * keep_rows
    for r in range(0, keep_rows, 8):
        keep = col_ids[:8] <= start + r + base_ids[:8]
        mine = pl.ds(pl.multiple_of(start + r, 8), 8)
        for i in range(comps):
            last_buffer[i, r : r + 8, :] = jnp.where(keep, buffer[i, mine, :], 0.0)
    going.append(pltpu.make_async_copy(last_buffer, last_ref, sent_last))
    going[-1].start()
    for copy in going:
        copy.wait()


def split(history, keep_rows, resident):
    comps, rows, cols = history.shape
    orbitals = comps // 2
    chunk = 5 if rows % 80 == 0 else 1
    part = (2, rows, cols)
    places = [near_out if i in resident else far_out for i in range(2 * orbitals)]
    specs = [pl.BlockSpec(memory_space=pltpu.VMEM if i in resident else pl.ANY) for i in range(2 * orbitals)]
    anywhere = pl.BlockSpec(memory_space=pl.ANY)
    *parts, last = pl.pallas_call(
        functools.partial(split_kernel, resident),
        out_shape=(*[place(part, jnp.bfloat16) for place in places], far_out((comps, keep_rows, cols))),
        in_specs=[anywhere],
        out_specs=(*specs, anywhere),
        scratch_shapes=[
            pltpu.VMEM(history.shape, jnp.float32),
            *[pltpu.VMEM(part, jnp.bfloat16)] * (2 * orbitals - len(resident)),
            pltpu.VMEM((comps, keep_rows, cols), jnp.float32),
            pltpu.SemaphoreType.DMA((chunk,)),
            pltpu.SemaphoreType.DMA((chunk, 2 * orbitals)),
            pltpu.SemaphoreType.DMA(()),
        ],
        compiler_params=pltpu.CompilerParams(vmem_limit_bytes=VMEM_LIMIT),
        name="split",
    )(far(history))
    return parts, last


def block_kernel(block, windows, stacked, step_size, factor_ref, sigma_ref, *refs):
    near_keys, far_keys = part_keys()
    held = dict(zip(near_keys, refs[: len(near_keys)], strict=True))
    refs = refs[len(near_keys) :]
    count = len(far_keys) + (1 if stacked else 2) + 2 * windows
    sources, outs, buffers = refs[:count], refs[count : -(count + 3)], refs[-(count + 3) : -3]
    arrived, sigma_scratch, joined = refs[-3:]
    piece_ref, outs = outs[-1], outs[:-1]
    held.update(zip(far_keys, buffers[: len(far_keys)], strict=True))
    rows_at = len(far_keys)
    previous = (buffers[rows_at].at[0], buffers[rows_at].at[1]) if stacked else buffers[rows_at : rows_at + 2]
    mine_refs, theirs_refs = buffers[count - 2 * windows : count - windows], buffers[count - windows :]
    comps, rows, cols = previous[0].shape
    orbitals = comps // 2
    known_rows = held[far_keys[0]].shape[1]
    used = known_rows + windows * 2 * rows
    wide = cols // LANES
    per_orbital = piece_ref.shape[0] // orbitals

    def part_of(ref, orbital):
        span = pl.ds(2 * orbital, 2)
        return ref.at[span] if len(ref.shape) == 3 else ref.at[:, span]

    known_copies, row_copies = {}, []
    for o in range(orbitals):
        for i, key in enumerate(far_keys):
            if key[1] == o:
                known_copies[key] = pltpu.make_async_copy(sources[i], buffers[i], arrived.at[o, i])
                known_copies[key].start()
        row_copies.append([
            pltpu.make_async_copy(part_of(sources[i], o), part_of(buffers[i], o), arrived.at[o, i])
            for i in range(rows_at, count)
        ])
        for copy in row_copies[o]:
            copy.start()
    core = lax.axis_index(CORE)
    mine_at = pl.ds(pl.multiple_of(core * rows, 8), rows)
    theirs_at = pl.ds(pl.multiple_of((1 - core) * rows, 8), rows)
    top = lax.broadcasted_iota(jnp.int32, (8, LANES), 0) < SUB
    row_ids = known_rows + block * 2 * rows + core * rows + lax.broadcasted_iota(jnp.int32, (rows, cols), 0)
    keep = lax.axis_index("tm") * cols + lax.broadcasted_iota(jnp.int32, (rows, cols), 1) <= row_ids

    def product(span, high, low):
        both = jnp.dot(sigma_scratch[:, span], high, preferred_element_type=jnp.float32)
        rest = jnp.dot(sigma_scratch[: 2 * rows, span], low, preferred_element_type=jnp.float32)
        return both[: 2 * rows] + (both[2 * rows :] + rest)

    for orbital in range(orbitals):
        base = orbital * per_orbital
        for tile in range(pl.cdiv(used, LANES)):
            shard, h = tile // wide, tile % wide
            reals, imags = [], []
            for pair in range(rows // 8):
                first = sigma_ref[shard, base + (2 * pair) * wide + h]
                second = sigma_ref[shard, base + (2 * pair + 1) * wide + h]
                reals.append(jnp.where(top, first, jnp.roll(second, SUB, 0)))
                imags.append(jnp.where(top, jnp.roll(first, SUB, 0), second))
            high, low = halves_of(jnp.concatenate(reals + imags, 0))
            lanes = slice(LANES * tile, LANES * tile + LANES)
            sigma_scratch[: 2 * rows, lanes] = high
            sigma_scratch[2 * rows :, lanes] = low

        for key, copy in known_copies.items():
            if key[1] == orbital:
                copy.wait()
        for copy in row_copies[orbital]:
            copy.wait()
        totals = None
        for momentum in range(2):
            keys = [(momentum, orbital, half) for half in range(2)]
            products = []
            for part in range(2):
                products.append(product(slice(0, known_rows), held[keys[0]][part], held[keys[1]][part]))
            for part in range(2):
                for window in range(windows):
                    joined[mine_at, :] = mine_refs[window][momentum, 2 * orbital + part]
                    joined[theirs_at, :] = theirs_refs[window][1 - momentum, 2 * orbital + part]
                    start = known_rows + window * 2 * rows
                    products[part] += product(slice(start, start + 2 * rows), *halves_of(joined[...]))
            by_real, by_imag = products
            x_re = previous[momentum][2 * orbital] + step_size * (by_real[:rows] - by_imag[rows:])
            x_im = previous[momentum][2 * orbital + 1] + step_size * (by_imag[:rows] + by_real[rows:])
            p_re = factor_ref[block, orbital, :, momentum : momentum + 1]
            p_im = factor_ref[block, orbital, :, 2 + momentum : 3 + momentum]
            real = jnp.where(keep, p_re * x_re - p_im * x_im, 0.0)
            imag = jnp.where(keep, p_re * x_im + p_im * x_re, 0.0)
            out = outs[0].at[momentum] if len(outs) == 1 else outs[momentum]
            out[2 * orbital] = real
            out[2 * orbital + 1] = imag
            totals = (real, imag) if totals is None else (totals[0] + real, totals[1] + imag)

        def store(index, tile, base=base):
            piece_ref[base + index] = tile

        store_packed(store, *totals)


RESIDENT = ((0, 1), (0,))


def part_keys():
    keys = [(m, o, half) for o in range(2) for m in range(2) for half in range(2)]
    here = [key for key in keys if 2 * key[1] + key[2] in RESIDENT[key[0]]]
    return here, [key for key in keys if key not in here]


def advance(block, last, step_size, sigma, factors, known, previous, mine, theirs):
    comps, rows, cols = previous[0].shape[-3:]
    known_rows = known[0][0].shape[1]
    used = pl.cdiv(known_rows + len(mine) * 2 * rows, LANES) * LANES
    near_keys, far_keys = part_keys()
    part = lambda key: known[key[0]][2 * key[1] + key[2]]
    sources = [*map(part, far_keys), *previous, *mine, *theirs]
    greens = [far_out((comps, rows, cols))] * 2 if last else [far_out((2, comps, rows, cols))]
    vmem = pl.BlockSpec(memory_space=pltpu.VMEM)
    *greens, pieces = pl.pallas_call(
        functools.partial(block_kernel, block, len(mine), len(previous) == 1, step_size),
        out_shape=(*greens, near_out((sigma.shape[1], 8, LANES))),
        in_specs=[vmem] * (2 + len(near_keys)) + [pl.BlockSpec(memory_space=pl.ANY)] * len(sources),
        out_specs=(vmem,) * (len(greens) + 1),
        scratch_shapes=[
            *[pltpu.VMEM(source.shape, source.dtype) for source in sources],
            pltpu.SemaphoreType.DMA((comps // 2, len(sources))),
            pltpu.VMEM((4 * rows, used), jnp.bfloat16),
            pltpu.VMEM((2 * rows, cols), jnp.float32),
        ],
        compiler_params=pltpu.CompilerParams(vmem_limit_bytes=VMEM_LIMIT),
    )(factors, near(sigma), *[near(part(key)) for key in near_keys], *[far(source) for source in sources])
    return greens, pieces


def cube_kernel(norm_factor, parts_ref, out_ref):
    sums = [parts_ref[i] for i in range(4)]
    for i in range(4, parts_ref.shape[0]):
        sums[i % 4] = sums[i % 4] + parts_ref[i]
    local = ((sums[0] + sums[1]) + (sums[2] + sums[3])) * norm_factor
    paired = jnp.roll(local, SUB, 0)
    value = 0.1 * (local * local * local - 3.0 * local * paired * paired)
    top = lax.broadcasted_iota(jnp.int32, local.shape, 0) < SUB
    value = jnp.where(top, value, -value)
    for i in range(out_ref.shape[0]):
        out_ref[i] = value


def cube(parts, norm_factor):
    kernel = functools.partial(cube_kernel, norm_factor)
    return call(kernel, [parts], [near_out(parts.shape)])[0]


def copies_kernel(value_ref, out_ref, sent):
    for copy in send_copies(value_ref, out_ref, sent, 0, pl.ds(0, value_ref.shape[0])):
        copy.wait()


def copies_of(value, count):
    return pl.pallas_call(
        copies_kernel,
        out_shape=far_out((count, *value.shape)),
        in_specs=[pl.BlockSpec(memory_space=pltpu.VMEM)],
        out_specs=pl.BlockSpec(memory_space=pl.ANY),
        scratch_shapes=[pltpu.SemaphoreType.DMA((1, count))],
        compiler_params=pltpu.CompilerParams(vmem_limit_bytes=VMEM_LIMIT),
        name="copies",
    )(near(value))


def green_kernel(mine_ref, theirs_ref, out_ref):
    rows = mine_ref.shape[1]
    core = lax.axis_index(CORE)
    out_ref[:, pl.ds(pl.multiple_of(core * rows, 8), rows), :] = mine_ref[...]
    out_ref[:, pl.ds(pl.multiple_of((1 - core) * rows, 8), rows), :] = theirs_ref[...]


def sigma_kernel(mine_ref, theirs_ref, out_ref):
    comps, rows, cols = out_ref.shape
    rows = rows // 2
    wide = cols // LANES
    core = lax.axis_index(CORE)
    top = lax.broadcasted_iota(jnp.int32, (8, LANES), 0) < SUB
    per_orbital = mine_ref.shape[0] // (comps // 2)
    for start, ref in ((core * rows, mine_ref), ((1 - core) * rows, theirs_ref)):
        for orbital in range(comps // 2):
            for pair in range(rows // 8):
                at = pl.ds(pl.multiple_of(start + 8 * pair, 8), 8)
                for h in range(wide):
                    first = ref[orbital * per_orbital + (2 * pair) * wide + h]
                    second = ref[orbital * per_orbital + (2 * pair + 1) * wide + h]
                    lanes = slice(LANES * h, LANES * h + LANES)
                    out_ref[2 * orbital, at, lanes] = jnp.where(top, first, jnp.roll(second, SUB, 0))
                    out_ref[2 * orbital + 1, at, lanes] = jnp.where(top, jnp.roll(first, SUB, 0), second)


def body(history, sigma_first, propagator):
    history, propagator = history[:, 0], propagator[:, 0]
    comps, _, cols = history.shape
    rows_block = sigma_first.shape[1]
    blocks = propagator.shape[1] // rows_block
    rows = rows_block // 2
    shards = lax.axis_size("tm")
    step_size = 1.0 / float(cols * shards) ** 0.5
    norm_factor = 1.0 / float(lax.axis_size(YZ) * lax.axis_size(CORE)) ** 0.5
    core = lax.axis_index(CORE)

    def swapped(value):
        return lax.ppermute(value, CORE, [(0, 1), (1, 0)])

    packed_first = pack(sigma_first, shards)
    sigma = lax.all_to_all(packed_first, "tm", 0, 0, tiled=True)
    their_history = swapped(history)
    their_propagator = swapped(propagator)
    known, greens = zip(split(history, rows, RESIDENT[0]), split(their_history, rows, RESIDENT[1]), strict=True)
    factors = jnp.stack([propagator, their_propagator]).reshape(2, comps // 2, 2, blocks, 2, rows)
    factors = lax.dynamic_index_in_dim(factors, core, 4, keepdims=False)
    factors = factors.transpose(3, 1, 4, 2, 0).reshape(blocks, comps // 2, rows, 4)
    mine, theirs = [], []
    for block in range(blocks):
        last = block + 1 == blocks
        greens, pieces = advance(block, last, step_size, sigma, factors, known, greens, mine, theirs)
        parts = lax.all_to_all(pieces, YZ, 0, 0, tiled=True)
        sigma = lax.all_to_all(cube(parts, norm_factor), YZ, 0, 0, tiled=True)
        if not last:
            mine.append(greens[0])
            theirs.append(swapped(greens[0]))
            sigma = lax.all_to_all(copies_of(sigma, shards), "tm", 0, 0, tiled=True)
    whole = [far_out((comps, rows_block, cols))]
    green_last = call(green_kernel, [greens[0], swapped(greens[1])], whole)[0]
    sigma_next = call(sigma_kernel, [sigma, swapped(sigma)], whole)[0]
    return green_last[:, None], sigma_next


def solution(mesh):
    torus = Mesh(mesh.devices.reshape(*GRID, mesh.shape["tm"]), (*YZ, CORE, "tm"))
    moms = (*YZ, CORE)
    return jax.shard_map(
        body,
        mesh=torus,
        in_specs=(P(None, moms, None, "tm"), P(None, None, "tm"), P(None, moms, None)),
        out_specs=(P(None, moms, None, "tm"), P(None, None, "tm")),
        check_vma=False,
    )
```

```python
import functools
import math

import jax
import jax.numpy as jnp
from jax import lax
from jax.experimental import pallas as pl
from jax.experimental.pallas import tpu as pltpu
from jax.sharding import Mesh
from jax.sharding import PartitionSpec as P


GRID = (8, 8, 2)
CORE = "core_of_chip"
YZ = ("mom_0", "mom_1")
VMEM_LIMIT = 32 << 20
SUB = 4
LANES = 128


def near(value):
    return pltpu.with_memory_space_constraint(value, pltpu.VMEM)


def far(value):
    return pltpu.with_memory_space_constraint(value, pltpu.HBM)


def near_out(shape, dtype=jnp.float32):
    return pltpu.VMEM(shape, dtype)


def far_out(shape, dtype=jnp.float32):
    return pltpu.HBM(shape, dtype)


def call(kernel, inputs, outputs, scratch=()):
    vmem = pl.BlockSpec(memory_space=pltpu.VMEM)
    return pl.pallas_call(
        kernel,
        out_shape=tuple(outputs),
        in_specs=[vmem] * len(inputs),
        out_specs=(vmem,) * len(outputs),
        scratch_shapes=scratch,
        compiler_params=pltpu.CompilerParams(vmem_limit_bytes=VMEM_LIMIT),
    )(*[near(value) for value in inputs])


def halves_of(value):
    high = value.astype(jnp.bfloat16)
    return high, (value - high.astype(jnp.float32)).astype(jnp.bfloat16)


def packed(real, imag):
    top = lax.broadcasted_iota(jnp.int32, real.shape, 0) < SUB
    return jnp.where(top, real, jnp.roll(imag, SUB, 0)), jnp.where(top, jnp.roll(real, SUB, 0), imag)


def store_packed(store, real, imag):
    rows, cols = real.shape
    wide = cols // LANES
    for pair in range(rows // 8):
        for h in range(wide):
            window = (slice(8 * pair, 8 * pair + 8), slice(LANES * h, LANES * h + LANES))
            first, second = packed(real[window], imag[window])
            store((2 * pair) * wide + h, first)
            store((2 * pair + 1) * wide + h, second)


def send_copies(source, out_ref, sent, index, span):
    copies = [
        pltpu.make_async_copy(source.at[span], out_ref.at[copy, span], sent.at[index, copy])
        for copy in range(out_ref.shape[0])
    ]
    for copy in copies:
        copy.start()
    return copies


def pack_kernel(sigma_ref, out_ref, piece_buffer, rows_buffer, arrived, sent):
    comps, rows = rows_buffer.shape[:2]
    per_orbital = piece_buffer.shape[0] // (comps // 2)
    mine = pl.ds(pl.multiple_of(lax.axis_index(CORE) * rows, 8), rows)
    coming = [
        pltpu.make_async_copy(sigma_ref.at[pl.ds(2 * o, 2), mine], rows_buffer.at[pl.ds(2 * o, 2)], arrived.at[o])
        for o in range(comps // 2)
    ]
    for copy in coming:
        copy.start()
    going = []
    for orbital in range(comps // 2):
        coming[orbital].wait()

        def store(index, tile, orbital=orbital):
            piece_buffer[orbital * per_orbital + index] = tile

        store_packed(store, rows_buffer[2 * orbital], rows_buffer[2 * orbital + 1])
        going += send_copies(piece_buffer, out_ref, sent, orbital, pl.ds(orbital * per_orbital, per_orbital))
    for copy in going:
        copy.wait()


def pack(sigma, copies):
    comps, rows, cols = sigma.shape
    pieces = comps // 2 * (rows // 2) * cols // (SUB * LANES)
    anywhere = pl.BlockSpec(memory_space=pl.ANY)
    return pl.pallas_call(
        pack_kernel,
        out_shape=(far_out((copies, pieces, 8, LANES)), near_out((pieces, 8, LANES))),
        in_specs=[anywhere],
        out_specs=(anywhere, pl.BlockSpec(memory_space=pltpu.VMEM)),
        scratch_shapes=[
            pltpu.VMEM((comps, rows // 2, cols), jnp.float32),
            pltpu.SemaphoreType.DMA((comps // 2,)),
            pltpu.SemaphoreType.DMA((comps // 2, copies)),
        ],
        compiler_params=pltpu.CompilerParams(vmem_limit_bytes=VMEM_LIMIT),
        name="pack",
    )(far(sigma))


def split_kernel(resident, history_ref, *refs):
    comps, rows, cols = history_ref.shape
    count = 2 * (comps // 2)
    outs, last_ref, held = refs[:count], refs[count], refs[count + 1 : count + 1 + len(resident)]
    buffer, *places, last_buffer, arrived, sent, sent_last = refs[count + 1 + len(resident) :]
    keep_rows = last_ref.shape[1]
    chunk = arrived.shape[0]
    step = rows // chunk
    coming = []
    for c in range(chunk):
        span = (slice(None), pl.ds(c * step, step))
        coming.append(pltpu.make_async_copy(history_ref.at[span], buffer.at[span], arrived.at[c]))
        coming[-1].start()
    col_ids = lax.axis_index("tm") * cols + lax.broadcasted_iota(jnp.int32, (16, cols), 1)
    base_ids = lax.broadcasted_iota(jnp.int32, (16, cols), 0)
    going = []
    for c in range(chunk):
        coming[c].wait()
        for r in range(c * step, (c + 1) * step, 16):
            keep = col_ids <= r + base_ids
            for i in range(comps):
                for n, value in enumerate(halves_of(jnp.where(keep, buffer[i, r : r + 16, :], 0.0))):
                    part = 2 * (i // 2) + n
                    places[part][i % 2, r : r + 16, :] = value
                    if part in resident and r >= cols:
                        held[resident.index(part)][i % 2, r - cols : r - cols + 16, :] = value
        for i in range(count):
            span = (slice(None), pl.ds(c * step, step))
            going.append(pltpu.make_async_copy(places[i].at[span], outs[i].at[span], sent.at[c, i]))
            going[-1].start()
    start = rows - 2 * keep_rows + lax.axis_index(CORE) * keep_rows
    for r in range(0, keep_rows, 8):
        keep = col_ids[:8] <= start + r + base_ids[:8]
        mine = pl.ds(pl.multiple_of(start + r, 8), 8)
        for i in range(comps):
            last_buffer[i, r : r + 8, :] = jnp.where(keep, buffer[i, mine, :], 0.0)
    going.append(pltpu.make_async_copy(last_buffer, last_ref, sent_last))
    going[-1].start()
    for copy in going:
        copy.wait()


def split(history, keep_rows, resident):
    comps, rows, cols = history.shape
    count = 2 * (comps // 2)
    chunk = 5 if rows % 80 == 0 else 1
    part, later = (2, rows, cols), (2, rows - cols, cols)
    anywhere = pl.BlockSpec(memory_space=pl.ANY)
    outs = pl.pallas_call(
        functools.partial(split_kernel, resident),
        out_shape=(
            *[far_out(part, jnp.bfloat16)] * count,
            far_out((comps, keep_rows, cols)),
            *[near_out(later, jnp.bfloat16)] * len(resident),
        ),
        in_specs=[anywhere],
        out_specs=(*[anywhere] * (count + 1), *[pl.BlockSpec(memory_space=pltpu.VMEM)] * len(resident)),
        scratch_shapes=[
            pltpu.VMEM(history.shape, jnp.float32),
            *[pltpu.VMEM(part, jnp.bfloat16)] * count,
            pltpu.VMEM((comps, keep_rows, cols), jnp.float32),
            pltpu.SemaphoreType.DMA((chunk,)),
            pltpu.SemaphoreType.DMA((chunk, count)),
            pltpu.SemaphoreType.DMA(()),
        ],
        compiler_params=pltpu.CompilerParams(vmem_limit_bytes=VMEM_LIMIT),
        name="split",
    )(far(history))
    return outs[:count], outs[count], dict(zip(resident, outs[count + 1 :], strict=True))


def unpack(load, scratch, rows, tile, lanes, wide, drop=None):
    top = lax.broadcasted_iota(jnp.int32, (8, LANES), 0) < SUB
    reals, imags = [], []
    for pair in range(rows // 8):
        first = load((2 * pair) * wide + tile % wide)
        second = load((2 * pair + 1) * wide + tile % wide)
        reals.append(jnp.where(top, first, jnp.roll(second, SUB, 0)))
        imags.append(jnp.where(top, jnp.roll(first, SUB, 0), second))
    value = jnp.concatenate(reals + imags, 0)
    if drop is not None:
        value = jnp.where(drop, 0.0, value)
    high, low = halves_of(value)
    scratch[: 2 * rows, lanes] = high
    scratch[2 * rows :, lanes] = low


def product(scratch, rows, span, high, low):
    both = jnp.dot(scratch[:, span], high, preferred_element_type=jnp.float32)
    rest = jnp.dot(scratch[: 2 * rows, span], low, preferred_element_type=jnp.float32)
    return both[: 2 * rows] + (both[2 * rows :] + rest)


def combined(by_real, by_imag, rows):
    return by_real[:rows] - by_imag[rows:], by_imag[:rows] + by_real[rows:]


def begin_kernel(stacked, step_size, sigma_ref, *refs):
    sources, refs = refs[:8], refs[8:]
    row_sources, refs = (refs[:1], refs[1:]) if stacked else (refs[:2], refs[2:])
    out_ref, buffers, row_buffer, sigma_scratch, arrived, rows_arrived = refs[0], refs[1:9], *refs[9:]
    _, comps, rows, cols = row_buffer.shape
    known_rows = sources[0].shape[1]
    piece = math.gcd(known_rows, cols)
    wide = cols // LANES
    per_orbital = sigma_ref.shape[0] // (comps // 2)
    first_row = lax.axis_index("tm") * cols
    if stacked:
        row_copies = [pltpu.make_async_copy(row_sources[0], row_buffer, rows_arrived.at[0])]
    else:
        row_copies = [
            pltpu.make_async_copy(source, row_buffer.at[m], rows_arrived.at[m]) for m, source in enumerate(row_sources)
        ]
    for copy in row_copies:
        copy.start()

    def copy_of(i, c):
        at = pl.ds(pl.multiple_of(first_row + c * piece, 16), piece)
        return pltpu.make_async_copy(sources[i].at[:, at], buffers[i].at[:, pl.ds(c * piece, piece)], arrived.at[i, c])

    for c in range(cols // piece):
        inside = first_row + c * piece < known_rows

        @pl.when(inside)
        def _(c=c):
            for i in range(8):
                copy_of(i, c).start()

        @pl.when(jnp.logical_not(inside))
        def _(c=c):
            for i in range(8):
                buffers[i][:, c * piece : (c + 1) * piece, :] = jnp.zeros((2, piece, cols), jnp.bfloat16)

    for c in range(cols // piece):

        @pl.when(first_row + c * piece < known_rows)
        def _(c=c):
            for i in range(8):
                copy_of(i, c).wait()

    for copy in row_copies:
        copy.wait()
    for orbital in range(comps // 2):
        for tile in range(wide):
            lanes = slice(LANES * tile, LANES * tile + LANES)
            unpack(lambda i, at=orbital * per_orbital: sigma_ref[at + i], sigma_scratch, rows, tile, lanes, wide)
        for momentum in range(2):
            high, low = buffers[4 * momentum + 2 * orbital : 4 * momentum + 2 * orbital + 2]
            products = [product(sigma_scratch, rows, slice(0, cols), high[part], low[part]) for part in range(2)]
            for part, value in enumerate(combined(*products, rows)):
                i = 2 * orbital + part
                out_ref[momentum, i] = row_buffer[momentum, i] + step_size * value


def begin(step_size, sigma, known, previous):
    comps, rows, cols = previous[0].shape[-3:]
    sources = [array for parts in known for array in parts]
    anywhere, vmem = pl.BlockSpec(memory_space=pl.ANY), pl.BlockSpec(memory_space=pltpu.VMEM)
    return pl.pallas_call(
        functools.partial(begin_kernel, len(previous) == 1, step_size),
        out_shape=far_out((2, comps, rows, cols)),
        in_specs=[vmem, *[anywhere] * (len(sources) + len(previous))],
        out_specs=vmem,
        scratch_shapes=[
            *[pltpu.VMEM((2, cols, cols), jnp.bfloat16)] * len(sources),
            pltpu.VMEM((2, comps, rows, cols), jnp.float32),
            pltpu.VMEM((4 * rows, cols), jnp.bfloat16),
            pltpu.SemaphoreType.DMA((len(sources), cols // math.gcd(sources[0].shape[1], cols))),
            pltpu.SemaphoreType.DMA((2,)),
        ],
        compiler_params=pltpu.CompilerParams(vmem_limit_bytes=VMEM_LIMIT),
        name="begin",
    )(near(sigma), *[far(value) for value in (*sources, *previous)])


def block_kernel(block, windows, known_rows, step_size, factor_ref, sigma_ref, *refs):
    near_keys, far_keys = part_keys()
    held = dict(zip(near_keys, refs[: len(near_keys)], strict=True))
    refs = refs[len(near_keys) :]
    count = len(far_keys) + 1 + 2 * windows
    sources, outs, buffers = refs[:count], refs[count : -(count + 3)], refs[-(count + 3) : -3]
    arrived, sigma_scratch, joined = refs[-3:]
    piece_ref, outs = outs[-1], outs[:-1]
    held.update(zip(far_keys, buffers[: len(far_keys)], strict=True))
    rows_at = len(far_keys)
    base_ref = buffers[rows_at]
    mine_refs, theirs_refs = buffers[count - 2 * windows : count - windows], buffers[count - windows :]
    _, comps, rows, cols = base_ref.shape
    orbitals = comps // 2
    used = known_rows + windows * 2 * rows
    wide = cols // LANES
    per_orbital = piece_ref.shape[0] // orbitals
    copies = []
    for o in range(orbitals):
        copies.append([
            pltpu.make_async_copy(sources[i].at[:, pl.ds(cols, known_rows - cols)], buffers[i], arrived.at[o, i])
            for i, key in enumerate(far_keys)
            if key[1] == o
        ] + [
            pltpu.make_async_copy(sources[i].at[:, pl.ds(2 * o, 2)], buffers[i].at[:, pl.ds(2 * o, 2)], arrived.at[o, i])
            for i in range(rows_at, count)
        ])
        for copy in copies[o]:
            copy.start()
    core, here = lax.axis_index(CORE), lax.axis_index("tm")
    mine_at = pl.ds(pl.multiple_of(core * rows, 8), rows)
    theirs_at = pl.ds(pl.multiple_of((1 - core) * rows, 8), rows)
    row_ids = known_rows + block * 2 * rows + core * rows + lax.broadcasted_iota(jnp.int32, (rows, cols), 0)
    keep = here * cols + lax.broadcasted_iota(jnp.int32, (rows, cols), 1) <= row_ids

    for orbital in range(orbitals):
        base = orbital * per_orbital
        for tile in range(wide, pl.cdiv(used, LANES)):
            start, shard = LANES * tile, tile // wide
            drop = None
            if start < known_rows:
                ids = start + lax.broadcasted_iota(jnp.int32, (4 * rows // 2, LANES), 1)
                drop = jnp.logical_and(here == shard, ids < known_rows)
            lanes = slice(start - cols, start - cols + LANES)
            unpack(lambda i, at=base, j=shard: sigma_ref[j, at + i], sigma_scratch, rows, tile, lanes, wide, drop)
        for copy in copies[orbital]:
            copy.wait()

        totals = None
        for momentum in range(2):
            products = []
            for part in range(2):
                high, low = (held[momentum, orbital, half][part] for half in range(2))
                total = product(sigma_scratch, rows, slice(0, known_rows - cols), high, low)
                for window in range(windows):
                    joined[mine_at, :] = mine_refs[window][momentum, 2 * orbital + part]
                    joined[theirs_at, :] = theirs_refs[window][1 - momentum, 2 * orbital + part]
                    start = known_rows - cols + window * 2 * rows
                    total += product(sigma_scratch, rows, slice(start, start + 2 * rows), *halves_of(joined[...]))
                products.append(total)
            real, imag = combined(*products, rows)
            x_re = base_ref[momentum, 2 * orbital] + step_size * real
            x_im = base_ref[momentum, 2 * orbital + 1] + step_size * imag
            p_re = factor_ref[block, orbital, :, momentum : momentum + 1]
            p_im = factor_ref[block, orbital, :, 2 + momentum : 3 + momentum]
            real = jnp.where(keep, p_re * x_re - p_im * x_im, 0.0)
            imag = jnp.where(keep, p_re * x_im + p_im * x_re, 0.0)
            out = outs[0].at[momentum] if len(outs) == 1 else outs[momentum]
            out[2 * orbital] = real
            out[2 * orbital + 1] = imag
            totals = (real, imag) if totals is None else (totals[0] + real, totals[1] + imag)

        def store(index, tile, base=base):
            piece_ref[base + index] = tile

        store_packed(store, *totals)


RESIDENT = ((0, 1, 2), (0, 1))


def part_keys():
    keys = [(m, o, half) for o in range(2) for m in range(2) for half in range(2)]
    here = [key for key in keys if 2 * key[1] + key[2] in RESIDENT[key[0]]]
    return here, [key for key in keys if key not in here]


def advance(block, last, step_size, sigma, factors, known, held, base, mine, theirs):
    _, comps, rows, cols = base.shape
    known_rows = known[0][0].shape[1]
    used = pl.cdiv(known_rows + len(mine) * 2 * rows, LANES) * LANES
    near_keys, far_keys = part_keys()
    far_parts = [known[m][2 * o + half] for m, o, half in far_keys]
    near_parts = [held[m][2 * o + half] for m, o, half in near_keys]
    sources = [*far_parts, base, *mine, *theirs]
    greens = [far_out((comps, rows, cols))] * 2 if last else [far_out((2, comps, rows, cols))]
    vmem = pl.BlockSpec(memory_space=pltpu.VMEM)
    *greens, pieces = pl.pallas_call(
        functools.partial(block_kernel, block, len(mine), known_rows, step_size),
        out_shape=(*greens, near_out((sigma.shape[1], 8, LANES))),
        in_specs=[vmem] * (2 + len(near_keys)) + [pl.BlockSpec(memory_space=pl.ANY)] * len(sources),
        out_specs=(vmem,) * (len(greens) + 1),
        scratch_shapes=[
            *[pltpu.VMEM((2, known_rows - cols, cols), jnp.bfloat16)] * len(far_parts),
            *[pltpu.VMEM(source.shape, source.dtype) for source in sources[len(far_parts) :]],
            pltpu.SemaphoreType.DMA((comps // 2, len(sources))),
            pltpu.VMEM((4 * rows, used - cols), jnp.bfloat16),
            pltpu.VMEM((2 * rows, cols), jnp.float32),
        ],
        compiler_params=pltpu.CompilerParams(vmem_limit_bytes=VMEM_LIMIT),
    )(factors, near(sigma), *map(near, near_parts), *map(far, sources))
    return greens, pieces


def cube_kernel(norm_factor, parts_ref, out_ref):
    sums = [parts_ref[i] for i in range(4)]
    for i in range(4, parts_ref.shape[0]):
        sums[i % 4] = sums[i % 4] + parts_ref[i]
    local = ((sums[0] + sums[1]) + (sums[2] + sums[3])) * norm_factor
    paired = jnp.roll(local, SUB, 0)
    value = 0.1 * (local * local * local - 3.0 * local * paired * paired)
    top = lax.broadcasted_iota(jnp.int32, local.shape, 0) < SUB
    value = jnp.where(top, value, -value)
    for i in range(out_ref.shape[0]):
        out_ref[i] = value


def cube(parts, norm_factor):
    kernel = functools.partial(cube_kernel, norm_factor)
    return call(kernel, [parts], [near_out(parts.shape)])[0]


def copies_kernel(value_ref, out_ref, sent):
    for copy in send_copies(value_ref, out_ref, sent, 0, pl.ds(0, value_ref.shape[0])):
        copy.wait()


def copies_of(value, count):
    return pl.pallas_call(
        copies_kernel,
        out_shape=far_out((count, *value.shape)),
        in_specs=[pl.BlockSpec(memory_space=pltpu.VMEM)],
        out_specs=pl.BlockSpec(memory_space=pl.ANY),
        scratch_shapes=[pltpu.SemaphoreType.DMA((1, count))],
        compiler_params=pltpu.CompilerParams(vmem_limit_bytes=VMEM_LIMIT),
        name="copies",
    )(near(value))


def green_kernel(mine_ref, theirs_ref, out_ref):
    rows = mine_ref.shape[1]
    core = lax.axis_index(CORE)
    out_ref[:, pl.ds(pl.multiple_of(core * rows, 8), rows), :] = mine_ref[...]
    out_ref[:, pl.ds(pl.multiple_of((1 - core) * rows, 8), rows), :] = theirs_ref[...]


def sigma_kernel(mine_ref, theirs_ref, out_ref):
    comps, rows, cols = out_ref.shape
    rows = rows // 2
    wide = cols // LANES
    core = lax.axis_index(CORE)
    top = lax.broadcasted_iota(jnp.int32, (8, LANES), 0) < SUB
    per_orbital = mine_ref.shape[0] // (comps // 2)
    for start, ref in ((core * rows, mine_ref), ((1 - core) * rows, theirs_ref)):
        for orbital in range(comps // 2):
            for pair in range(rows // 8):
                at = pl.ds(pl.multiple_of(start + 8 * pair, 8), 8)
                for h in range(wide):
                    first = ref[orbital * per_orbital + (2 * pair) * wide + h]
                    second = ref[orbital * per_orbital + (2 * pair + 1) * wide + h]
                    lanes = slice(LANES * h, LANES * h + LANES)
                    out_ref[2 * orbital, at, lanes] = jnp.where(top, first, jnp.roll(second, SUB, 0))
                    out_ref[2 * orbital + 1, at, lanes] = jnp.where(top, jnp.roll(first, SUB, 0), second)


def body(history, sigma_first, propagator):
    history, propagator = history[:, 0], propagator[:, 0]
    comps, _, cols = history.shape
    rows_block = sigma_first.shape[1]
    blocks = propagator.shape[1] // rows_block
    rows = rows_block // 2
    shards = lax.axis_size("tm")
    step_size = 1.0 / float(cols * shards) ** 0.5
    norm_factor = 1.0 / float(lax.axis_size(YZ) * lax.axis_size(CORE)) ** 0.5
    core = lax.axis_index(CORE)

    def swapped(value):
        return lax.ppermute(value, CORE, [(0, 1), (1, 0)])

    packed_first, sigma_cols = pack(sigma_first, shards)
    sigma = lax.all_to_all(packed_first, "tm", 0, 0, tiled=True)
    their_history = swapped(history)
    their_propagator = swapped(propagator)
    known, greens, held = zip(split(history, rows, RESIDENT[0]), split(their_history, rows, RESIDENT[1]), strict=True)
    factors = jnp.stack([propagator, their_propagator]).reshape(2, comps // 2, 2, blocks, 2, rows)
    factors = lax.dynamic_index_in_dim(factors, core, 4, keepdims=False)
    factors = factors.transpose(3, 1, 4, 2, 0).reshape(blocks, comps // 2, rows, 4)
    mine, theirs = [], []
    for block in range(blocks):
        last = block + 1 == blocks
        base = begin(step_size, sigma_cols, known, greens)
        greens, pieces = advance(block, last, step_size, sigma, factors, known, held, base, mine, theirs)
        parts = lax.all_to_all(pieces, YZ, 0, 0, tiled=True)
        sigma_cols = lax.all_to_all(cube(parts, norm_factor), YZ, 0, 0, tiled=True)
        if not last:
            mine.append(greens[0])
            theirs.append(swapped(greens[0]))
            sigma = lax.all_to_all(copies_of(sigma_cols, shards), "tm", 0, 0, tiled=True)
    whole = [far_out((comps, rows_block, cols))]
    green_last = call(green_kernel, [greens[0], swapped(greens[1])], whole)[0]
    green_last, sigma_cols = lax.optimization_barrier((green_last, sigma_cols))
    sigma_next = call(sigma_kernel, [sigma_cols, swapped(sigma_cols)], whole)[0]
    return green_last[:, None], sigma_next


def solution(mesh):
    torus = Mesh(mesh.devices.reshape(*GRID, mesh.shape["tm"]), (*YZ, CORE, "tm"))
    moms = (*YZ, CORE)
    return jax.shard_map(
        body,
        mesh=torus,
        in_specs=(P(None, moms, None, "tm"), P(None, None, "tm"), P(None, moms, None)),
        out_specs=(P(None, moms, None, "tm"), P(None, None, "tm")),
        check_vma=False,
    )
```

```python
import functools
import math

import jax
import jax.numpy as jnp
from jax import lax
from jax.experimental import pallas as pl
from jax.experimental.pallas import tpu as pltpu
from jax.sharding import Mesh
from jax.sharding import PartitionSpec as P


GRID = (8, 8, 2)
CORE = "core_of_chip"
YZ = ("mom_0", "mom_1")
VMEM_LIMIT = 32 << 20
SUB = 4
LANES = 128


def near(value):
    return pltpu.with_memory_space_constraint(value, pltpu.VMEM)


def far(value):
    return pltpu.with_memory_space_constraint(value, pltpu.HBM)


def near_out(shape, dtype=jnp.float32):
    return pltpu.VMEM(shape, dtype)


def far_out(shape, dtype=jnp.float32):
    return pltpu.HBM(shape, dtype)


def call(kernel, inputs, outputs, scratch=()):
    vmem = pl.BlockSpec(memory_space=pltpu.VMEM)
    return pl.pallas_call(
        kernel,
        out_shape=tuple(outputs),
        in_specs=[vmem] * len(inputs),
        out_specs=(vmem,) * len(outputs),
        scratch_shapes=scratch,
        compiler_params=pltpu.CompilerParams(vmem_limit_bytes=VMEM_LIMIT),
    )(*[near(value) for value in inputs])


def halves_of(value):
    high = value.astype(jnp.bfloat16)
    return high, (value - high.astype(jnp.float32)).astype(jnp.bfloat16)


def packed(real, imag):
    top = lax.broadcasted_iota(jnp.int32, real.shape, 0) < SUB
    return jnp.where(top, real, jnp.roll(imag, SUB, 0)), jnp.where(top, jnp.roll(real, SUB, 0), imag)


def store_packed(store, real, imag):
    rows, cols = real.shape
    wide = cols // LANES
    for pair in range(rows // 8):
        for h in range(wide):
            window = (slice(8 * pair, 8 * pair + 8), slice(LANES * h, LANES * h + LANES))
            first, second = packed(real[window], imag[window])
            store((2 * pair) * wide + h, first)
            store((2 * pair + 1) * wide + h, second)


def send_copies(source, out_ref, sent, index, span):
    copies = [
        pltpu.make_async_copy(source.at[span], out_ref.at[copy, span], sent.at[index, copy])
        for copy in range(out_ref.shape[0])
    ]
    for copy in copies:
        copy.start()
    return copies


def pack_kernel(sigma_ref, out_ref, piece_buffer, rows_buffer, arrived, sent):
    comps, rows = rows_buffer.shape[:2]
    per_orbital = piece_buffer.shape[0] // (comps // 2)
    mine = pl.ds(pl.multiple_of(lax.axis_index(CORE) * rows, 8), rows)
    coming = [
        pltpu.make_async_copy(sigma_ref.at[pl.ds(2 * o, 2), mine], rows_buffer.at[pl.ds(2 * o, 2)], arrived.at[o])
        for o in range(comps // 2)
    ]
    for copy in coming:
        copy.start()
    going = []
    for orbital in range(comps // 2):
        coming[orbital].wait()

        def store(index, tile, orbital=orbital):
            piece_buffer[orbital * per_orbital + index] = tile

        store_packed(store, rows_buffer[2 * orbital], rows_buffer[2 * orbital + 1])
        going += send_copies(piece_buffer, out_ref, sent, orbital, pl.ds(orbital * per_orbital, per_orbital))
    for copy in going:
        copy.wait()


def pack(sigma, copies):
    comps, rows, cols = sigma.shape
    pieces = comps // 2 * (rows // 2) * cols // (SUB * LANES)
    anywhere = pl.BlockSpec(memory_space=pl.ANY)
    return pl.pallas_call(
        pack_kernel,
        out_shape=(far_out((copies, pieces, 8, LANES)), near_out((pieces, 8, LANES))),
        in_specs=[anywhere],
        out_specs=(anywhere, pl.BlockSpec(memory_space=pltpu.VMEM)),
        scratch_shapes=[
            pltpu.VMEM((comps, rows // 2, cols), jnp.float32),
            pltpu.SemaphoreType.DMA((comps // 2,)),
            pltpu.SemaphoreType.DMA((comps // 2, copies)),
        ],
        compiler_params=pltpu.CompilerParams(vmem_limit_bytes=VMEM_LIMIT),
        name="pack",
    )(far(sigma))


def split_kernel(resident, history_ref, *refs):
    comps, rows, cols = history_ref.shape
    count = 2 * (comps // 2)
    outs, last_ref, held = refs[:count], refs[count], refs[count + 1 : count + 1 + len(resident)]
    buffer, *places, last_buffer, arrived, sent, sent_last = refs[count + 1 + len(resident) :]
    keep_rows = last_ref.shape[1]
    chunk = arrived.shape[0]
    step = rows // chunk
    coming = []
    for c in range(chunk):
        span = (slice(None), pl.ds(c * step, step))
        coming.append(pltpu.make_async_copy(history_ref.at[span], buffer.at[span], arrived.at[c]))
        coming[-1].start()
    col_ids = lax.axis_index("tm") * cols + lax.broadcasted_iota(jnp.int32, (16, cols), 1)
    base_ids = lax.broadcasted_iota(jnp.int32, (16, cols), 0)
    going = []
    for c in range(chunk):
        coming[c].wait()
        for r in range(c * step, (c + 1) * step, 16):
            keep = col_ids <= r + base_ids
            for i in range(comps):
                for n, value in enumerate(halves_of(jnp.where(keep, buffer[i, r : r + 16, :], 0.0))):
                    part = 2 * (i // 2) + n
                    places[part][i % 2, r : r + 16, :] = value
                    if part in resident and r >= cols:
                        held[resident.index(part)][i % 2, r - cols : r - cols + 16, :] = value
        for i in range(count):
            span = (slice(None), pl.ds(c * step, step))
            going.append(pltpu.make_async_copy(places[i].at[span], outs[i].at[span], sent.at[c, i]))
            going[-1].start()
    start = rows - 2 * keep_rows + lax.axis_index(CORE) * keep_rows
    for r in range(0, keep_rows, 8):
        keep = col_ids[:8] <= start + r + base_ids[:8]
        mine = pl.ds(pl.multiple_of(start + r, 8), 8)
        for i in range(comps):
            last_buffer[i, r : r + 8, :] = jnp.where(keep, buffer[i, mine, :], 0.0)
    going.append(pltpu.make_async_copy(last_buffer, last_ref, sent_last))
    going[-1].start()
    for copy in going:
        copy.wait()


def split(history, keep_rows, resident):
    comps, rows, cols = history.shape
    count = 2 * (comps // 2)
    chunk = 5 if rows % 80 == 0 else 1
    part, later = (2, rows, cols), (2, rows - cols, cols)
    anywhere = pl.BlockSpec(memory_space=pl.ANY)
    outs = pl.pallas_call(
        functools.partial(split_kernel, resident),
        out_shape=(
            *[far_out(part, jnp.bfloat16)] * count,
            far_out((comps, keep_rows, cols)),
            *[near_out(later, jnp.bfloat16)] * len(resident),
        ),
        in_specs=[anywhere],
        out_specs=(*[anywhere] * (count + 1), *[pl.BlockSpec(memory_space=pltpu.VMEM)] * len(resident)),
        scratch_shapes=[
            pltpu.VMEM(history.shape, jnp.float32),
            *[pltpu.VMEM(part, jnp.bfloat16)] * count,
            pltpu.VMEM((comps, keep_rows, cols), jnp.float32),
            pltpu.SemaphoreType.DMA((chunk,)),
            pltpu.SemaphoreType.DMA((chunk, count)),
            pltpu.SemaphoreType.DMA(()),
        ],
        compiler_params=pltpu.CompilerParams(vmem_limit_bytes=VMEM_LIMIT),
        name="split",
    )(far(history))
    return outs[:count], outs[count], dict(zip(resident, outs[count + 1 :], strict=True))


def unpack(load, scratch, rows, tile, lanes, wide, drop=None):
    top = lax.broadcasted_iota(jnp.int32, (8, LANES), 0) < SUB
    reals, imags = [], []
    for pair in range(rows // 8):
        first = load((2 * pair) * wide + tile % wide)
        second = load((2 * pair + 1) * wide + tile % wide)
        reals.append(jnp.where(top, first, jnp.roll(second, SUB, 0)))
        imags.append(jnp.where(top, jnp.roll(first, SUB, 0), second))
    value = jnp.concatenate(reals + imags, 0)
    if drop is not None:
        value = jnp.where(drop, 0.0, value)
    high, low = halves_of(value)
    scratch[: 2 * rows, lanes] = high
    scratch[2 * rows :, lanes] = low


def product(scratch, rows, span, high, low):
    both = jnp.dot(scratch[:, span], high, preferred_element_type=jnp.float32)
    rest = jnp.dot(scratch[: 2 * rows, span], low, preferred_element_type=jnp.float32)
    return both[: 2 * rows] + (both[2 * rows :] + rest)


def combined(by_real, by_imag, rows):
    return by_real[:rows] - by_imag[rows:], by_imag[:rows] + by_real[rows:]


def begin_kernel(stacked, step_size, sigma_ref, *refs):
    sources, refs = refs[:8], refs[8:]
    row_sources, refs = (refs[:1], refs[1:]) if stacked else (refs[:2], refs[2:])
    out_ref, buffers, row_buffer, sigma_scratch, arrived, rows_arrived = refs[0], refs[1:9], *refs[9:]
    _, comps, rows, cols = row_buffer.shape
    known_rows = sources[0].shape[1]
    piece = math.gcd(known_rows, cols)
    wide = cols // LANES
    per_orbital = sigma_ref.shape[0] // (comps // 2)
    first_row = lax.axis_index("tm") * cols
    if stacked:
        row_copies = [pltpu.make_async_copy(row_sources[0], row_buffer, rows_arrived.at[0])]
    else:
        row_copies = [
            pltpu.make_async_copy(source, row_buffer.at[m], rows_arrived.at[m]) for m, source in enumerate(row_sources)
        ]
    for copy in row_copies:
        copy.start()

    def copy_of(i, c):
        at = pl.ds(pl.multiple_of(first_row + c * piece, 16), piece)
        return pltpu.make_async_copy(sources[i].at[:, at], buffers[i].at[:, pl.ds(c * piece, piece)], arrived.at[i, c])

    for c in range(cols // piece):
        inside = first_row + c * piece < known_rows

        @pl.when(inside)
        def _(c=c):
            for i in range(8):
                copy_of(i, c).start()

        @pl.when(jnp.logical_not(inside))
        def _(c=c):
            for i in range(8):
                buffers[i][:, c * piece : (c + 1) * piece, :] = jnp.zeros((2, piece, cols), jnp.bfloat16)

    for c in range(cols // piece):

        @pl.when(first_row + c * piece < known_rows)
        def _(c=c):
            for i in range(8):
                copy_of(i, c).wait()

    for copy in row_copies:
        copy.wait()
    for orbital in range(comps // 2):
        for tile in range(wide):
            lanes = slice(LANES * tile, LANES * tile + LANES)
            unpack(lambda i, at=orbital * per_orbital: sigma_ref[at + i], sigma_scratch, rows, tile, lanes, wide)
        for momentum in range(2):
            high, low = buffers[4 * momentum + 2 * orbital : 4 * momentum + 2 * orbital + 2]
            products = [product(sigma_scratch, rows, slice(0, cols), high[part], low[part]) for part in range(2)]
            for part, value in enumerate(combined(*products, rows)):
                i = 2 * orbital + part
                out_ref[momentum, i] = row_buffer[momentum, i] + step_size * value


def begin(step_size, sigma, known, previous):
    comps, rows, cols = previous[0].shape[-3:]
    sources = [array for parts in known for array in parts]
    anywhere, vmem = pl.BlockSpec(memory_space=pl.ANY), pl.BlockSpec(memory_space=pltpu.VMEM)
    return pl.pallas_call(
        functools.partial(begin_kernel, len(previous) == 1, step_size),
        out_shape=far_out((2, comps, rows, cols)),
        in_specs=[vmem, *[anywhere] * (len(sources) + len(previous))],
        out_specs=vmem,
        scratch_shapes=[
            *[pltpu.VMEM((2, cols, cols), jnp.bfloat16)] * len(sources),
            pltpu.VMEM((2, comps, rows, cols), jnp.float32),
            pltpu.VMEM((4 * rows, cols), jnp.bfloat16),
            pltpu.SemaphoreType.DMA((len(sources), cols // math.gcd(sources[0].shape[1], cols))),
            pltpu.SemaphoreType.DMA((2,)),
        ],
        compiler_params=pltpu.CompilerParams(vmem_limit_bytes=VMEM_LIMIT),
        name="begin",
    )(near(sigma), *[far(value) for value in (*sources, *previous)])


def block_kernel(block, windows, known_rows, whole, step_size, factor_ref, sigma_ref, *refs):
    near_keys, far_keys = part_keys()
    held = dict(zip(near_keys, refs[: len(near_keys)], strict=True))
    refs = refs[len(near_keys) :]
    count = len(far_keys) + 1 + 2 * windows
    if whole:
        pair, parts, refs = refs[:2], refs[2:10], refs[10:]
        *refs, arrived_first, arrived_pair = refs
        firsts, refs = refs[-8:], refs[:-8]
    sources, outs, buffers = refs[:count], refs[count : -(count + 3)], refs[-(count + 3) : -3]
    arrived, sigma_scratch, joined = refs[-3:]
    piece_ref, outs = outs[-1], outs[:-1]
    held.update(zip(far_keys, buffers[: len(far_keys)], strict=True))
    rows_at = len(far_keys)
    base_ref = buffers[rows_at]
    mine_refs, theirs_refs = buffers[count - 2 * windows : count - windows], buffers[count - windows :]
    _, comps, rows, cols = base_ref.shape
    orbitals = comps // 2
    used = known_rows + windows * 2 * rows
    wide = cols // LANES
    per_orbital = piece_ref.shape[0] // orbitals
    copies = []
    for o in range(orbitals):
        copies.append([
            pltpu.make_async_copy(sources[i].at[:, pl.ds(cols, known_rows - cols)], buffers[i], arrived.at[o, i])
            for i, key in enumerate(far_keys)
            if key[1] == o
        ] + [
            pltpu.make_async_copy(sources[i].at[:, pl.ds(2 * o, 2)], buffers[i].at[:, pl.ds(2 * o, 2)], arrived.at[o, i])
            for i in range(rows_at + whole, count)
        ])
        if whole:
            span = pl.ds(2 * o, 2)
            for m in range(2):
                copies[o].append(pltpu.make_async_copy(pair[m].at[span], base_ref.at[m, span], arrived_pair.at[o, m]))
                for i in (4 * m + 2 * o, 4 * m + 2 * o + 1):
                    copies[o].append(pltpu.make_async_copy(parts[i].at[:, pl.ds(0, cols)], firsts[i], arrived_first.at[i]))
        for copy in copies[o]:
            copy.start()
    core, here = lax.axis_index(CORE), lax.axis_index("tm")
    mine_at = pl.ds(pl.multiple_of(core * rows, 8), rows)
    theirs_at = pl.ds(pl.multiple_of((1 - core) * rows, 8), rows)
    row_ids = known_rows + block * 2 * rows + core * rows + lax.broadcasted_iota(jnp.int32, (rows, cols), 0)
    keep = here * cols + lax.broadcasted_iota(jnp.int32, (rows, cols), 1) <= row_ids

    for orbital in range(orbitals):
        base = orbital * per_orbital
        skipped = 0 if whole else cols
        for tile in range(skipped // LANES, pl.cdiv(used, LANES)):
            start, shard = LANES * tile, tile // wide
            drop = None
            if start < known_rows and not whole:
                ids = start + lax.broadcasted_iota(jnp.int32, (4 * rows // 2, LANES), 1)
                drop = jnp.logical_and(here == shard, ids < known_rows)
            lanes = slice(start - skipped, start - skipped + LANES)
            unpack(lambda i, at=base, j=shard: sigma_ref[j, at + i], sigma_scratch, rows, tile, lanes, wide, drop)
        for copy in copies[orbital]:
            copy.wait()

        totals = None
        for momentum in range(2):
            products = []
            for part in range(2):
                high, low = (held[momentum, orbital, half][part] for half in range(2))
                total = product(sigma_scratch, rows, slice(cols - skipped, known_rows - skipped), high, low)
                if whole:
                    high, low = (firsts[4 * momentum + 2 * orbital + half][part] for half in range(2))
                    total += product(sigma_scratch, rows, slice(0, cols), high, low)
                for window in range(windows):
                    joined[mine_at, :] = mine_refs[window][momentum, 2 * orbital + part]
                    joined[theirs_at, :] = theirs_refs[window][1 - momentum, 2 * orbital + part]
                    start = known_rows - skipped + window * 2 * rows
                    total += product(sigma_scratch, rows, slice(start, start + 2 * rows), *halves_of(joined[...]))
                products.append(total)
            real, imag = combined(*products, rows)
            x_re = base_ref[momentum, 2 * orbital] + step_size * real
            x_im = base_ref[momentum, 2 * orbital + 1] + step_size * imag
            p_re = factor_ref[block, orbital, :, momentum : momentum + 1]
            p_im = factor_ref[block, orbital, :, 2 + momentum : 3 + momentum]
            real = jnp.where(keep, p_re * x_re - p_im * x_im, 0.0)
            imag = jnp.where(keep, p_re * x_im + p_im * x_re, 0.0)
            out = outs[0].at[momentum] if len(outs) == 1 else outs[momentum]
            out[2 * orbital] = real
            out[2 * orbital + 1] = imag
            totals = (real, imag) if totals is None else (totals[0] + real, totals[1] + imag)

        def store(index, tile, base=base):
            piece_ref[base + index] = tile

        store_packed(store, *totals)


RESIDENT = ((0, 1, 2), (0, 1))


def part_keys():
    keys = [(m, o, half) for o in range(2) for m in range(2) for half in range(2)]
    here = [key for key in keys if 2 * key[1] + key[2] in RESIDENT[key[0]]]
    return here, [key for key in keys if key not in here]


def advance(block, last, step_size, sigma, factors, known, held, base, mine, theirs):
    whole = len(base) == 2
    comps, rows, cols = base[0].shape[-3:]
    known_rows = known[0][0].shape[1]
    used = pl.cdiv(known_rows + len(mine) * 2 * rows, LANES) * LANES
    near_keys, far_keys = part_keys()
    far_parts = [known[m][2 * o + half] for m, o, half in far_keys]
    near_parts = [held[m][2 * o + half] for m, o, half in near_keys]
    sources = [*far_parts, base[0], *mine, *theirs]
    extra = [*base, *known[0], *known[1]] if whole else []
    greens = [far_out((comps, rows, cols))] * 2 if last else [far_out((2, comps, rows, cols))]
    vmem = pl.BlockSpec(memory_space=pltpu.VMEM)
    *greens, pieces = pl.pallas_call(
        functools.partial(block_kernel, block, len(mine), known_rows, whole, step_size),
        out_shape=(*greens, near_out((sigma.shape[1], 8, LANES))),
        in_specs=[vmem] * (2 + len(near_keys)) + [pl.BlockSpec(memory_space=pl.ANY)] * (len(sources) + len(extra)),
        out_specs=(vmem,) * (len(greens) + 1),
        scratch_shapes=[
            *[pltpu.VMEM((2, known_rows - cols, cols), jnp.bfloat16)] * len(far_parts),
            *[pltpu.VMEM((2, comps, rows, cols), jnp.float32)] * (1 + 2 * len(mine)),
            pltpu.SemaphoreType.DMA((comps // 2, len(sources))),
            pltpu.VMEM((4 * rows, used if whole else used - cols), jnp.bfloat16),
            pltpu.VMEM((2 * rows, cols), jnp.float32),
            *([pltpu.VMEM((2, cols, cols), jnp.bfloat16)] * 8 if whole else []),
            *([pltpu.SemaphoreType.DMA((8,)), pltpu.SemaphoreType.DMA((comps // 2, 2))] if whole else []),
        ],
        compiler_params=pltpu.CompilerParams(vmem_limit_bytes=VMEM_LIMIT),
    )(factors, near(sigma), *map(near, near_parts), *map(far, extra), *map(far, sources))
    return greens, pieces


def cube_kernel(norm_factor, parts_ref, out_ref):
    sums = [parts_ref[i] for i in range(4)]
    for i in range(4, parts_ref.shape[0]):
        sums[i % 4] = sums[i % 4] + parts_ref[i]
    local = ((sums[0] + sums[1]) + (sums[2] + sums[3])) * norm_factor
    paired = jnp.roll(local, SUB, 0)
    value = 0.1 * (local * local * local - 3.0 * local * paired * paired)
    top = lax.broadcasted_iota(jnp.int32, local.shape, 0) < SUB
    value = jnp.where(top, value, -value)
    for i in range(out_ref.shape[0]):
        out_ref[i] = value


def cube(parts, norm_factor):
    kernel = functools.partial(cube_kernel, norm_factor)
    return call(kernel, [parts], [near_out(parts.shape)])[0]


def copies_kernel(value_ref, out_ref, sent):
    for copy in send_copies(value_ref, out_ref, sent, 0, pl.ds(0, value_ref.shape[0])):
        copy.wait()


def copies_of(value, count):
    return pl.pallas_call(
        copies_kernel,
        out_shape=far_out((count, *value.shape)),
        in_specs=[pl.BlockSpec(memory_space=pltpu.VMEM)],
        out_specs=pl.BlockSpec(memory_space=pl.ANY),
        scratch_shapes=[pltpu.SemaphoreType.DMA((1, count))],
        compiler_params=pltpu.CompilerParams(vmem_limit_bytes=VMEM_LIMIT),
        name="copies",
    )(near(value))


def green_kernel(mine_ref, theirs_ref, out_ref):
    rows = mine_ref.shape[1]
    core = lax.axis_index(CORE)
    out_ref[:, pl.ds(pl.multiple_of(core * rows, 8), rows), :] = mine_ref[...]
    out_ref[:, pl.ds(pl.multiple_of((1 - core) * rows, 8), rows), :] = theirs_ref[...]


def sigma_kernel(mine_ref, theirs_ref, out_ref):
    comps, rows, cols = out_ref.shape
    rows = rows // 2
    wide = cols // LANES
    core = lax.axis_index(CORE)
    top = lax.broadcasted_iota(jnp.int32, (8, LANES), 0) < SUB
    per_orbital = mine_ref.shape[0] // (comps // 2)
    for start, ref in ((core * rows, mine_ref), ((1 - core) * rows, theirs_ref)):
        for orbital in range(comps // 2):
            for pair in range(rows // 8):
                at = pl.ds(pl.multiple_of(start + 8 * pair, 8), 8)
                for h in range(wide):
                    first = ref[orbital * per_orbital + (2 * pair) * wide + h]
                    second = ref[orbital * per_orbital + (2 * pair + 1) * wide + h]
                    lanes = slice(LANES * h, LANES * h + LANES)
                    out_ref[2 * orbital, at, lanes] = jnp.where(top, first, jnp.roll(second, SUB, 0))
                    out_ref[2 * orbital + 1, at, lanes] = jnp.where(top, jnp.roll(first, SUB, 0), second)


def body(history, sigma_first, propagator):
    history, propagator = history[:, 0], propagator[:, 0]
    comps, _, cols = history.shape
    rows_block = sigma_first.shape[1]
    blocks = propagator.shape[1] // rows_block
    rows = rows_block // 2
    shards = lax.axis_size("tm")
    step_size = 1.0 / float(cols * shards) ** 0.5
    norm_factor = 1.0 / float(lax.axis_size(YZ) * lax.axis_size(CORE)) ** 0.5
    core = lax.axis_index(CORE)

    def swapped(value):
        return lax.ppermute(value, CORE, [(0, 1), (1, 0)])

    packed_first, sigma_cols = pack(sigma_first, shards)
    sigma = lax.all_to_all(packed_first, "tm", 0, 0, tiled=True)
    their_history = swapped(history)
    their_propagator = swapped(propagator)
    known, greens, held = zip(split(history, rows, RESIDENT[0]), split(their_history, rows, RESIDENT[1]), strict=True)
    factors = jnp.stack([propagator, their_propagator]).reshape(2, comps // 2, 2, blocks, 2, rows)
    factors = lax.dynamic_index_in_dim(factors, core, 4, keepdims=False)
    factors = factors.transpose(3, 1, 4, 2, 0).reshape(blocks, comps // 2, rows, 4)
    mine, theirs = [], []
    for block in range(blocks):
        last = block + 1 == blocks
        base = [begin(step_size, sigma_cols, known, greens)] if block else greens
        greens, pieces = advance(block, last, step_size, sigma, factors, known, held, base, mine, theirs)
        parts = lax.all_to_all(pieces, YZ, 0, 0, tiled=True)
        sigma_cols = lax.all_to_all(cube(parts, norm_factor), YZ, 0, 0, tiled=True)
        if not last:
            mine.append(greens[0])
            theirs.append(swapped(greens[0]))
            sigma = lax.all_to_all(copies_of(sigma_cols, shards), "tm", 0, 0, tiled=True)
    whole = [far_out((comps, rows_block, cols))]
    green_last = call(green_kernel, [greens[0], swapped(greens[1])], whole)[0]
    green_last, sigma_cols = lax.optimization_barrier((green_last, sigma_cols))
    sigma_next = call(sigma_kernel, [sigma_cols, swapped(sigma_cols)], whole)[0]
    return green_last[:, None], sigma_next


def solution(mesh):
    torus = Mesh(mesh.devices.reshape(*GRID, mesh.shape["tm"]), (*YZ, CORE, "tm"))
    moms = (*YZ, CORE)
    return jax.shard_map(
        body,
        mesh=torus,
        in_specs=(P(None, moms, None, "tm"), P(None, None, "tm"), P(None, moms, None)),
        out_specs=(P(None, moms, None, "tm"), P(None, None, "tm")),
        check_vma=False,
    )
```

```python
import functools
import math

import jax
import jax.numpy as jnp
from jax import lax
from jax.experimental import pallas as pl
from jax.experimental.pallas import tpu as pltpu
from jax.sharding import Mesh
from jax.sharding import PartitionSpec as P


GRID = (8, 8, 2)
CORE = "core_of_chip"
YZ = ("mom_0", "mom_1")
VMEM_LIMIT = 32 << 20
SUB = 4
LANES = 128


def near(value):
    return pltpu.with_memory_space_constraint(value, pltpu.VMEM)


def far(value):
    return pltpu.with_memory_space_constraint(value, pltpu.HBM)


def near_out(shape, dtype=jnp.float32):
    return pltpu.VMEM(shape, dtype)


def far_out(shape, dtype=jnp.float32):
    return pltpu.HBM(shape, dtype)


def call(kernel, inputs, outputs, scratch=()):
    vmem = pl.BlockSpec(memory_space=pltpu.VMEM)
    return pl.pallas_call(
        kernel,
        out_shape=tuple(outputs),
        in_specs=[vmem] * len(inputs),
        out_specs=(vmem,) * len(outputs),
        scratch_shapes=scratch,
        compiler_params=pltpu.CompilerParams(vmem_limit_bytes=VMEM_LIMIT),
    )(*[near(value) for value in inputs])


def halves_of(value):
    high = value.astype(jnp.bfloat16)
    return high, (value - high.astype(jnp.float32)).astype(jnp.bfloat16)


def packed(real, imag):
    top = lax.broadcasted_iota(jnp.int32, real.shape, 0) < SUB
    return jnp.where(top, real, jnp.roll(imag, SUB, 0)), jnp.where(top, jnp.roll(real, SUB, 0), imag)


def store_packed(store, real, imag):
    rows, cols = real.shape
    wide = cols // LANES
    for pair in range(rows // 8):
        for h in range(wide):
            window = (slice(8 * pair, 8 * pair + 8), slice(LANES * h, LANES * h + LANES))
            first, second = packed(real[window], imag[window])
            store((2 * pair) * wide + h, first)
            store((2 * pair + 1) * wide + h, second)


def send_copies(source, out_ref, sent, index, span):
    copies = [
        pltpu.make_async_copy(source.at[span], out_ref.at[copy, span], sent.at[index, copy])
        for copy in range(out_ref.shape[0])
    ]
    for copy in copies:
        copy.start()
    return copies


def pack_kernel(sigma_ref, out_ref, rows_buffer, piece_buffer, arrived, sent):
    comps, rows = rows_buffer.shape[:2]
    per_orbital = piece_buffer.shape[0] // (comps // 2)
    mine = pl.ds(pl.multiple_of(lax.axis_index(CORE) * rows, 8), rows)
    coming = [
        pltpu.make_async_copy(sigma_ref.at[pl.ds(2 * o, 2), mine], rows_buffer.at[pl.ds(2 * o, 2)], arrived.at[o])
        for o in range(comps // 2)
    ]
    for copy in coming:
        copy.start()
    going = []
    for orbital in range(comps // 2):
        coming[orbital].wait()

        def store(index, tile, orbital=orbital):
            piece_buffer[orbital * per_orbital + index] = tile

        store_packed(store, rows_buffer[2 * orbital], rows_buffer[2 * orbital + 1])
        going += send_copies(piece_buffer, out_ref, sent, orbital, pl.ds(orbital * per_orbital, per_orbital))
    for copy in going:
        copy.wait()


def pack(sigma, copies):
    comps, rows, cols = sigma.shape
    pieces = comps // 2 * (rows // 2) * cols // (SUB * LANES)
    anywhere = pl.BlockSpec(memory_space=pl.ANY)
    return pl.pallas_call(
        pack_kernel,
        out_shape=far_out((copies, pieces, 8, LANES)),
        in_specs=[anywhere],
        out_specs=anywhere,
        scratch_shapes=[
            pltpu.VMEM((comps, rows // 2, cols), jnp.float32),
            pltpu.VMEM((pieces, 8, LANES), jnp.float32),
            pltpu.SemaphoreType.DMA((comps // 2,)),
            pltpu.SemaphoreType.DMA((comps // 2, copies)),
        ],
        compiler_params=pltpu.CompilerParams(vmem_limit_bytes=VMEM_LIMIT),
        name="pack",
    )(far(sigma))


def split_kernel(resident, history_ref, *refs):
    comps, rows, cols = history_ref.shape
    count = 2 * (comps // 2)
    outs, last_ref, held = refs[:count], refs[count], refs[count + 1 : count + 1 + len(resident)]
    buffer, *places, last_buffer, arrived, sent, sent_last = refs[count + 1 + len(resident) :]
    keep_rows = last_ref.shape[1]
    chunk = arrived.shape[0]
    step = rows // chunk
    coming = []
    for c in range(chunk):
        span = (slice(None), pl.ds(c * step, step))
        coming.append(pltpu.make_async_copy(history_ref.at[span], buffer.at[span], arrived.at[c]))
        coming[-1].start()
    col_ids = lax.axis_index("tm") * cols + lax.broadcasted_iota(jnp.int32, (16, cols), 1)
    base_ids = lax.broadcasted_iota(jnp.int32, (16, cols), 0)
    going = []
    for c in range(chunk):
        coming[c].wait()
        for r in range(c * step, (c + 1) * step, 16):
            keep = col_ids <= r + base_ids
            for i in range(comps):
                for n, value in enumerate(halves_of(jnp.where(keep, buffer[i, r : r + 16, :], 0.0))):
                    part = 2 * (i // 2) + n
                    places[part][i % 2, r : r + 16, :] = value
                    if part in resident and r >= cols:
                        held[resident.index(part)][i % 2, r - cols : r - cols + 16, :] = value
        for i in range(count):
            span = (slice(None), pl.ds(c * step, step))
            going.append(pltpu.make_async_copy(places[i].at[span], outs[i].at[span], sent.at[c, i]))
            going[-1].start()
    start = rows - 2 * keep_rows + lax.axis_index(CORE) * keep_rows
    for r in range(0, keep_rows, 8):
        keep = col_ids[:8] <= start + r + base_ids[:8]
        mine = pl.ds(pl.multiple_of(start + r, 8), 8)
        for i in range(comps):
            last_buffer[i, r : r + 8, :] = jnp.where(keep, buffer[i, mine, :], 0.0)
    going.append(pltpu.make_async_copy(last_buffer, last_ref, sent_last))
    going[-1].start()
    for copy in going:
        copy.wait()


def split(history, keep_rows, resident):
    comps, rows, cols = history.shape
    count = 2 * (comps // 2)
    chunk = 5 if rows % 80 == 0 else 1
    part, later = (2, rows, cols), (2, rows - cols, cols)
    anywhere = pl.BlockSpec(memory_space=pl.ANY)
    outs = pl.pallas_call(
        functools.partial(split_kernel, resident),
        out_shape=(
            *[far_out(part, jnp.bfloat16)] * count,
            far_out((comps, keep_rows, cols)),
            *[near_out(later, jnp.bfloat16)] * len(resident),
        ),
        in_specs=[anywhere],
        out_specs=(*[anywhere] * (count + 1), *[pl.BlockSpec(memory_space=pltpu.VMEM)] * len(resident)),
        scratch_shapes=[
            pltpu.VMEM(history.shape, jnp.float32),
            *[pltpu.VMEM(part, jnp.bfloat16)] * count,
            pltpu.VMEM((comps, keep_rows, cols), jnp.float32),
            pltpu.SemaphoreType.DMA((chunk,)),
            pltpu.SemaphoreType.DMA((chunk, count)),
            pltpu.SemaphoreType.DMA(()),
        ],
        compiler_params=pltpu.CompilerParams(vmem_limit_bytes=VMEM_LIMIT),
        name="split",
    )(far(history))
    return outs[:count], outs[count], dict(zip(resident, outs[count + 1 :], strict=True))


def unpack(load, scratch, rows, tile, lanes, wide, drop=None):
    top = lax.broadcasted_iota(jnp.int32, (8, LANES), 0) < SUB
    reals, imags = [], []
    for pair in range(rows // 8):
        first = load((2 * pair) * wide + tile % wide)
        second = load((2 * pair + 1) * wide + tile % wide)
        reals.append(jnp.where(top, first, jnp.roll(second, SUB, 0)))
        imags.append(jnp.where(top, jnp.roll(first, SUB, 0), second))
    value = jnp.concatenate(reals + imags, 0)
    if drop is not None:
        value = jnp.where(drop, 0.0, value)
    high, low = halves_of(value)
    scratch[: 2 * rows, lanes] = high
    scratch[2 * rows :, lanes] = low


def product(scratch, rows, span, high, low):
    both = jnp.dot(scratch[:, span], high, preferred_element_type=jnp.float32)
    rest = jnp.dot(scratch[: 2 * rows, span], low, preferred_element_type=jnp.float32)
    return both[: 2 * rows] + (both[2 * rows :] + rest)


def combined(by_real, by_imag, rows):
    return by_real[:rows] - by_imag[rows:], by_imag[:rows] + by_real[rows:]


def begin_kernel(stacked, step_size, sigma_ref, *refs):
    sources, refs = refs[:8], refs[8:]
    row_sources, refs = (refs[:1], refs[1:]) if stacked else (refs[:2], refs[2:])
    out_ref, buffers, row_buffer, sigma_scratch, arrived, rows_arrived = refs[0], refs[1:9], *refs[9:]
    _, comps, rows, cols = row_buffer.shape
    known_rows = sources[0].shape[1]
    piece = math.gcd(known_rows, cols)
    wide = cols // LANES
    per_orbital = sigma_ref.shape[0] // (comps // 2)
    first_row = lax.axis_index("tm") * cols
    if stacked:
        row_copies = [pltpu.make_async_copy(row_sources[0], row_buffer, rows_arrived.at[0])]
    else:
        row_copies = [
            pltpu.make_async_copy(source, row_buffer.at[m], rows_arrived.at[m]) for m, source in enumerate(row_sources)
        ]
    for copy in row_copies:
        copy.start()

    def copy_of(i, c):
        at = pl.ds(pl.multiple_of(first_row + c * piece, 16), piece)
        return pltpu.make_async_copy(sources[i].at[:, at], buffers[i].at[:, pl.ds(c * piece, piece)], arrived.at[i, c])

    for c in range(cols // piece):
        inside = first_row + c * piece < known_rows

        @pl.when(inside)
        def _(c=c):
            for i in range(8):
                copy_of(i, c).start()

        @pl.when(jnp.logical_not(inside))
        def _(c=c):
            for i in range(8):
                buffers[i][:, c * piece : (c + 1) * piece, :] = jnp.zeros((2, piece, cols), jnp.bfloat16)

    for c in range(cols // piece):

        @pl.when(first_row + c * piece < known_rows)
        def _(c=c):
            for i in range(8):
                copy_of(i, c).wait()

    for copy in row_copies:
        copy.wait()
    for orbital in range(comps // 2):
        for tile in range(wide):
            lanes = slice(LANES * tile, LANES * tile + LANES)
            unpack(lambda i, at=orbital * per_orbital: sigma_ref[at + i], sigma_scratch, rows, tile, lanes, wide)
        for momentum in range(2):
            high, low = buffers[4 * momentum + 2 * orbital : 4 * momentum + 2 * orbital + 2]
            products = [product(sigma_scratch, rows, slice(0, cols), high[part], low[part]) for part in range(2)]
            for part, value in enumerate(combined(*products, rows)):
                i = 2 * orbital + part
                out_ref[momentum, i] = row_buffer[momentum, i] + step_size * value


def begin(step_size, sigma, known, previous):
    comps, rows, cols = previous[0].shape[-3:]
    sources = [array for parts in known for array in parts]
    anywhere, vmem = pl.BlockSpec(memory_space=pl.ANY), pl.BlockSpec(memory_space=pltpu.VMEM)
    return pl.pallas_call(
        functools.partial(begin_kernel, len(previous) == 1, step_size),
        out_shape=far_out((2, comps, rows, cols)),
        in_specs=[vmem, *[anywhere] * (len(sources) + len(previous))],
        out_specs=vmem,
        scratch_shapes=[
            *[pltpu.VMEM((2, cols, cols), jnp.bfloat16)] * len(sources),
            pltpu.VMEM((2, comps, rows, cols), jnp.float32),
            pltpu.VMEM((4 * rows, cols), jnp.bfloat16),
            pltpu.SemaphoreType.DMA((len(sources), cols // math.gcd(sources[0].shape[1], cols))),
            pltpu.SemaphoreType.DMA((2,)),
        ],
        compiler_params=pltpu.CompilerParams(vmem_limit_bytes=VMEM_LIMIT),
        name="begin",
    )(near(sigma), *[far(value) for value in (*sources, *previous)])


def block_kernel(block, windows, known_rows, whole, step_size, factor_ref, sigma_ref, *refs):
    near_keys, far_keys = part_keys()
    held = dict(zip(near_keys, refs[: len(near_keys)], strict=True))
    refs = refs[len(near_keys) :]
    count = len(far_keys) + 1 + 2 * windows
    if whole:
        pair, parts, refs = refs[:2], refs[2:10], refs[10:]
        *refs, arrived_first, arrived_pair = refs
        firsts, refs = refs[-8:], refs[:-8]
    sources, outs, buffers = refs[:count], refs[count : -(count + 3)], refs[-(count + 3) : -3]
    arrived, sigma_scratch, joined = refs[-3:]
    piece_ref, outs = outs[-1], outs[:-1]
    held.update(zip(far_keys, buffers[: len(far_keys)], strict=True))
    rows_at = len(far_keys)
    base_ref = buffers[rows_at]
    mine_refs, theirs_refs = buffers[count - 2 * windows : count - windows], buffers[count - windows :]
    _, comps, rows, cols = base_ref.shape
    orbitals = comps // 2
    used = known_rows + windows * 2 * rows
    wide = cols // LANES
    per_orbital = piece_ref.shape[0] // orbitals
    copies = []
    for o in range(orbitals):
        copies.append([
            pltpu.make_async_copy(sources[i].at[:, pl.ds(cols, known_rows - cols)], buffers[i], arrived.at[o, i])
            for i, key in enumerate(far_keys)
            if key[1] == o
        ] + [
            pltpu.make_async_copy(sources[i].at[:, pl.ds(2 * o, 2)], buffers[i].at[:, pl.ds(2 * o, 2)], arrived.at[o, i])
            for i in range(rows_at + whole, count)
        ])
        if whole:
            span = pl.ds(2 * o, 2)
            for m in range(2):
                copies[o].append(pltpu.make_async_copy(pair[m].at[span], base_ref.at[m, span], arrived_pair.at[o, m]))
                for i in (4 * m + 2 * o, 4 * m + 2 * o + 1):
                    copies[o].append(pltpu.make_async_copy(parts[i].at[:, pl.ds(0, cols)], firsts[i], arrived_first.at[i]))
        for copy in copies[o]:
            copy.start()
    core, here = lax.axis_index(CORE), lax.axis_index("tm")
    mine_at = pl.ds(pl.multiple_of(core * rows, 8), rows)
    theirs_at = pl.ds(pl.multiple_of((1 - core) * rows, 8), rows)
    row_ids = known_rows + block * 2 * rows + core * rows + lax.broadcasted_iota(jnp.int32, (rows, cols), 0)
    keep = here * cols + lax.broadcasted_iota(jnp.int32, (rows, cols), 1) <= row_ids

    for orbital in range(orbitals):
        base = orbital * per_orbital
        skipped = 0 if whole else cols
        for tile in range(skipped // LANES, pl.cdiv(used, LANES)):
            start, shard = LANES * tile, tile // wide
            drop = None
            if start < known_rows and not whole:
                ids = start + lax.broadcasted_iota(jnp.int32, (4 * rows // 2, LANES), 1)
                drop = jnp.logical_and(here == shard, ids < known_rows)
            lanes = slice(start - skipped, start - skipped + LANES)
            unpack(lambda i, at=base, j=shard: sigma_ref[j, at + i], sigma_scratch, rows, tile, lanes, wide, drop)
        for copy in copies[orbital]:
            copy.wait()

        totals = None
        for momentum in range(2):
            products = []
            for part in range(2):
                high, low = (held[momentum, orbital, half][part] for half in range(2))
                total = product(sigma_scratch, rows, slice(cols - skipped, known_rows - skipped), high, low)
                if whole:
                    high, low = (firsts[4 * momentum + 2 * orbital + half][part] for half in range(2))
                    total += product(sigma_scratch, rows, slice(0, cols), high, low)
                for window in range(windows):
                    joined[mine_at, :] = mine_refs[window][momentum, 2 * orbital + part]
                    joined[theirs_at, :] = theirs_refs[window][1 - momentum, 2 * orbital + part]
                    start = known_rows - skipped + window * 2 * rows
                    total += product(sigma_scratch, rows, slice(start, start + 2 * rows), *halves_of(joined[...]))
                products.append(total)
            real, imag = combined(*products, rows)
            x_re = base_ref[momentum, 2 * orbital] + step_size * real
            x_im = base_ref[momentum, 2 * orbital + 1] + step_size * imag
            p_re = factor_ref[block, orbital, :, momentum : momentum + 1]
            p_im = factor_ref[block, orbital, :, 2 + momentum : 3 + momentum]
            real = jnp.where(keep, p_re * x_re - p_im * x_im, 0.0)
            imag = jnp.where(keep, p_re * x_im + p_im * x_re, 0.0)
            out = outs[0].at[momentum] if len(outs) == 1 else outs[momentum]
            out[2 * orbital] = real
            out[2 * orbital + 1] = imag
            totals = (real, imag) if totals is None else (totals[0] + real, totals[1] + imag)

        def store(index, tile, base=base):
            piece_ref[base + index] = tile

        store_packed(store, *totals)


RESIDENT = ((0, 1, 2), (0, 1))


def part_keys():
    keys = [(m, o, half) for o in range(2) for m in range(2) for half in range(2)]
    here = [key for key in keys if 2 * key[1] + key[2] in RESIDENT[key[0]]]
    return here, [key for key in keys if key not in here]


def advance(block, last, step_size, sigma, factors, known, held, base, mine, theirs):
    whole = len(base) == 2
    comps, rows, cols = base[0].shape[-3:]
    known_rows = known[0][0].shape[1]
    used = pl.cdiv(known_rows + len(mine) * 2 * rows, LANES) * LANES
    near_keys, far_keys = part_keys()
    far_parts = [known[m][2 * o + half] for m, o, half in far_keys]
    near_parts = [held[m][2 * o + half] for m, o, half in near_keys]
    sources = [*far_parts, base[0], *mine, *theirs]
    extra = [*base, *known[0], *known[1]] if whole else []
    greens = [far_out((comps, rows, cols))] * 2 if last else [far_out((2, comps, rows, cols))]
    vmem = pl.BlockSpec(memory_space=pltpu.VMEM)
    *greens, pieces = pl.pallas_call(
        functools.partial(block_kernel, block, len(mine), known_rows, whole, step_size),
        out_shape=(*greens, near_out((sigma.shape[1], 8, LANES))),
        in_specs=[vmem] * (2 + len(near_keys)) + [pl.BlockSpec(memory_space=pl.ANY)] * (len(sources) + len(extra)),
        out_specs=(vmem,) * (len(greens) + 1),
        scratch_shapes=[
            *[pltpu.VMEM((2, known_rows - cols, cols), jnp.bfloat16)] * len(far_parts),
            *[pltpu.VMEM((2, comps, rows, cols), jnp.float32)] * (1 + 2 * len(mine)),
            pltpu.SemaphoreType.DMA((comps // 2, len(sources))),
            pltpu.VMEM((4 * rows, used if whole else used - cols), jnp.bfloat16),
            pltpu.VMEM((2 * rows, cols), jnp.float32),
            *([pltpu.VMEM((2, cols, cols), jnp.bfloat16)] * 8 if whole else []),
            *([pltpu.SemaphoreType.DMA((8,)), pltpu.SemaphoreType.DMA((comps // 2, 2))] if whole else []),
        ],
        compiler_params=pltpu.CompilerParams(vmem_limit_bytes=VMEM_LIMIT),
    )(factors, near(sigma), *map(near, near_parts), *map(far, extra), *map(far, sources))
    return greens, pieces


def cube_kernel(norm_factor, parts_ref, out_ref):
    sums = [parts_ref[i] for i in range(4)]
    for i in range(4, parts_ref.shape[0]):
        sums[i % 4] = sums[i % 4] + parts_ref[i]
    local = ((sums[0] + sums[1]) + (sums[2] + sums[3])) * norm_factor
    paired = jnp.roll(local, SUB, 0)
    value = 0.1 * (local * local * local - 3.0 * local * paired * paired)
    top = lax.broadcasted_iota(jnp.int32, local.shape, 0) < SUB
    value = jnp.where(top, value, -value)
    for i in range(out_ref.shape[0]):
        out_ref[i] = value


def cube(parts, norm_factor):
    kernel = functools.partial(cube_kernel, norm_factor)
    return call(kernel, [parts], [near_out(parts.shape)])[0]


def copies_kernel(value_ref, out_ref, sent):
    for copy in send_copies(value_ref, out_ref, sent, 0, pl.ds(0, value_ref.shape[0])):
        copy.wait()


def copies_of(value, count):
    return pl.pallas_call(
        copies_kernel,
        out_shape=far_out((count, *value.shape)),
        in_specs=[pl.BlockSpec(memory_space=pltpu.VMEM)],
        out_specs=pl.BlockSpec(memory_space=pl.ANY),
        scratch_shapes=[pltpu.SemaphoreType.DMA((1, count))],
        compiler_params=pltpu.CompilerParams(vmem_limit_bytes=VMEM_LIMIT),
        name="copies",
    )(near(value))


def green_kernel(mine_ref, theirs_ref, out_ref):
    rows = mine_ref.shape[1]
    core = lax.axis_index(CORE)
    out_ref[:, pl.ds(pl.multiple_of(core * rows, 8), rows), :] = mine_ref[...]
    out_ref[:, pl.ds(pl.multiple_of((1 - core) * rows, 8), rows), :] = theirs_ref[...]


def sigma_kernel(mine_ref, theirs_ref, out_ref):
    comps, rows, cols = out_ref.shape
    rows = rows // 2
    wide = cols // LANES
    core = lax.axis_index(CORE)
    top = lax.broadcasted_iota(jnp.int32, (8, LANES), 0) < SUB
    per_orbital = mine_ref.shape[0] // (comps // 2)
    for start, ref in ((core * rows, mine_ref), ((1 - core) * rows, theirs_ref)):
        for orbital in range(comps // 2):
            for pair in range(rows // 8):
                at = pl.ds(pl.multiple_of(start + 8 * pair, 8), 8)
                for h in range(wide):
                    first = ref[orbital * per_orbital + (2 * pair) * wide + h]
                    second = ref[orbital * per_orbital + (2 * pair + 1) * wide + h]
                    lanes = slice(LANES * h, LANES * h + LANES)
                    out_ref[2 * orbital, at, lanes] = jnp.where(top, first, jnp.roll(second, SUB, 0))
                    out_ref[2 * orbital + 1, at, lanes] = jnp.where(top, jnp.roll(first, SUB, 0), second)


def body(history, sigma_first, propagator):
    history, propagator = history[:, 0], propagator[:, 0]
    comps, _, cols = history.shape
    rows_block = sigma_first.shape[1]
    blocks = propagator.shape[1] // rows_block
    rows = rows_block // 2
    shards = lax.axis_size("tm")
    step_size = 1.0 / float(cols * shards) ** 0.5
    norm_factor = 1.0 / float(lax.axis_size(YZ) * lax.axis_size(CORE)) ** 0.5
    core = lax.axis_index(CORE)

    def swapped(value):
        return lax.ppermute(value, CORE, [(0, 1), (1, 0)])

    packed_first, sigma_cols = pack(sigma_first, shards), None
    sigma = lax.all_to_all(packed_first, "tm", 0, 0, tiled=True)
    their_history = swapped(history)
    their_propagator = swapped(propagator)
    known, greens, held = zip(split(history, rows, RESIDENT[0]), split(their_history, rows, RESIDENT[1]), strict=True)
    factors = jnp.stack([propagator, their_propagator]).reshape(2, comps // 2, 2, blocks, 2, rows)
    factors = lax.dynamic_index_in_dim(factors, core, 4, keepdims=False)
    factors = factors.transpose(3, 1, 4, 2, 0).reshape(blocks, comps // 2, rows, 4)
    mine, theirs = [], []
    for block in range(blocks):
        last = block + 1 == blocks
        base = [begin(step_size, sigma_cols, known, greens)] if block else greens
        greens, pieces = advance(block, last, step_size, sigma, factors, known, held, base, mine, theirs)
        parts = lax.all_to_all(pieces, YZ, 0, 0, tiled=True)
        sigma_cols = lax.all_to_all(cube(parts, norm_factor), YZ, 0, 0, tiled=True)
        if not last:
            mine.append(greens[0])
            theirs.append(swapped(greens[0]))
            sigma = lax.all_to_all(copies_of(sigma_cols, shards), "tm", 0, 0, tiled=True)
    whole = [far_out((comps, rows_block, cols))]
    green_last = call(green_kernel, [greens[0], swapped(greens[1])], whole)[0]
    green_last, sigma_cols = lax.optimization_barrier((green_last, sigma_cols))
    sigma_next = call(sigma_kernel, [sigma_cols, swapped(sigma_cols)], whole)[0]
    return green_last[:, None], sigma_next


def solution(mesh):
    torus = Mesh(mesh.devices.reshape(*GRID, mesh.shape["tm"]), (*YZ, CORE, "tm"))
    moms = (*YZ, CORE)
    return jax.shard_map(
        body,
        mesh=torus,
        in_specs=(P(None, moms, None, "tm"), P(None, None, "tm"), P(None, moms, None)),
        out_specs=(P(None, moms, None, "tm"), P(None, None, "tm")),
        check_vma=False,
    )
```
